32 devices in a mesh: dp: 16 (over z, y, core), seq: 2 (over x).
Axes of the slice: x: 2, y: 2, z: 4, core: 2. Of those that a mesh axis runs over, the one named last changes fastest.
Arguments:
- tokens: bfloat16 [16, 1024, 1024], P('dp', 'seq'), may hold values from -6 to 6
- segment_ids: int32 [16, 1024], P('dp'), may hold values from 0 to 3, never falling along the last dimension, each value on 1 to 512 neighbouring positions
- norm1_gain: bfloat16 [1024], P(('dp', 'seq')), may hold values from 0.5 to 1.5
- w_mamba_in: bfloat16 [1024, 3328], P(('dp', 'seq')), may hold values from -0.1875 to 0.1875
- w_delta: bfloat16 [1024, 24], P(('dp', 'seq')), may hold values from -0.09375 to 0.09375
- conv_weight: bfloat16 [4, 1792], P(None, ('dp', 'seq')), may hold values from -3 to 3
- conv_bias: bfloat16 [1792], P(('dp', 'seq')), may hold values from -3 to 3
- delta_bias: bfloat16 [24], replicated, may hold values from -6 to -2
- decay_log: bfloat16 [24], replicated, may hold values from -1 to 1.5
- skip_gain: bfloat16 [24], replicated, may hold values from 0.5 to 1.5
- w_mamba_out: bfloat16 [1536, 1024], P(('dp', 'seq')), may hold values from -0.15625 to 0.15625
- w_qkv: bfloat16 [1024, 768], P(('dp', 'seq')), may hold values from -0.1875 to 0.1875
- w_attn_out: bfloat16 [512, 1024], P(('dp', 'seq')), may hold values from -0.75 to 0.75
- norm2_gain: bfloat16 [1024], P(('dp', 'seq')), may hold values from 0.5 to 1.5
- w_gate_up: bfloat16 [1024, 4096], P(('dp', 'seq')), may hold values from -0.1875 to 0.1875
- w_down: bfloat16 [2048, 1024], P(('dp', 'seq')), may hold values from -0.125 to 0.125
- cotangent: bfloat16 [16, 1024, 1024], P('dp', 'seq'), may hold values from -6 to 6
Outputs:
- block_out: bfloat16 [16, 1024, 1024], P('dp', 'seq')
- grad_tokens: float32 [16, 1024, 1024], P('dp', 'seq')
- grad_norm1_gain: float32 [1024], P(('dp', 'seq'))
- grad_w_mamba_in: float32 [1024, 3328], P(('dp', 'seq'))
- grad_w_delta: float32 [1024, 24], P(('dp', 'seq'))
- grad_conv_weight: float32 [4, 1792], P(None, ('dp', 'seq'))
- grad_conv_bias: float32 [1792], P(('dp', 'seq'))
- grad_delta_bias: float32 [24], replicated
- grad_decay_log: float32 [24], replicated
- grad_skip_gain: float32 [24], replicated
- grad_w_mamba_out: float32 [1536, 1024], P(('dp', 'seq'))
- grad_w_qkv: float32 [1024, 768], P(('dp', 'seq'))
- grad_w_attn_out: float32 [512, 1024], P(('dp', 'seq'))
- grad_norm2_gain: float32 [1024], P(('dp', 'seq'))
- grad_w_gate_up: float32 [1024, 4096], P(('dp', 'seq'))
- grad_w_down: float32 [2048, 1024], P(('dp', 'seq'))
The draws below stay inside these ranges and needn't reach their ends.
All inputs are finite; a program needn't handle non-finite values.
Results may differ from the reference program's by a relative error of at most 0.012.
Values may be sent and summed in bfloat16 or wider, within the bound.
No kernel may reach another device: no remote copies, remote signals or barrier semaphores. Data moves between devices by JAX's collectives and lax.ppermute only.
A program may use at most 256 MiB of HBM per device.

```python
import math
import jax
import jax.numpy as jnp
import numpy as np
from jax import lax

D = 1024
MHEADS = 24
MHDIM = 64
STATE = 128
CONVW = 4
AHEADS = 8
KVHEADS = 2
AHDIM = 64
FF = 2048
TOK_DEV = 512
SEQS = 16
LEN = 1024


def shard_levels(stream_key, shape, pieces, smallest, top_value):
    loudness, own = 1.0, jax.random.fold_in(stream_key, 6)
    for dim, shards_of in pieces:
        heights = jnp.exp(jax.random.uniform(jax.random.fold_in(own, dim), (shards_of,), jnp.float32, smallest / len(pieces), top_value / len(pieces)))
        loudness = loudness * jnp.repeat(heights, shape[dim] // shards_of).reshape([-1 if axis == dim else 1 for axis in range(len(shape))])
    return loudness


def profile(amount, total, bound, skew):
    loads = [(1 << 20) // math.isqrt(rank ** skew) + 1 for rank in range(2, amount + 1)]
    spare, holding = total - bound - (amount - 1), [1] * (amount - 1)
    while spare > 0:
        movable = [i for i in range(amount - 1) if holding[i] < bound]
        mass, budget = sum([loads[i] for i in movable]), spare
        for i in movable:
            addition = min(bound - holding[i], max(1, budget * loads[i] // mass), spare)
            holding[i] = holding[i] + addition
            spare = spare - addition
    return np.array([bound] + holding)


def uneven_parts(own_key, number_of, total, bound, slope):
    if number_of == 2:
        one = jax.random.randint(own_key, (), max(1, total - bound), min(bound, total - 1) + 1)
        return jnp.stack([one, total - one])
    tallies = jnp.asarray(profile(number_of, total, bound, slope), jnp.int32)
    couples = (number_of - 1) // 2
    giver, taker = tallies[1:1 + 2 * couples:2], tallies[2:2 + 2 * couples:2]
    margin = jnp.minimum(giver - 1, bound - taker)
    shifted = jax.random.randint(jax.random.fold_in(own_key, 1), (couples,), 0, 1 << 20) % (margin + 1)
    tallies = tallies.at[1:1 + 2 * couples:2].set(giver - shifted).at[2:2 + 2 * couples:2].set(taker + shifted)
    return tallies[jax.random.permutation(jax.random.fold_in(own_key, 2), number_of)]


def centred(own_key, shape, width, reach, split=(), kind=jnp.bfloat16):
    values = width * jax.random.normal(own_key, shape, jnp.float32)
    if split:
        values = values * shard_levels(own_key, shape, split, -0.22, 0.18)
    return jnp.clip(values, -reach, reach).astype(kind)


def setup_inputs(seed: int = 0) -> dict:
    streams_of = jax.random.split(jax.random.key(seed), 18)
    return {
        "tokens": centred(streams_of[0], (SEQS, LEN, D), 1.0, 6.0, ((0, 16), (1, 2))),
        "segment_ids": jax.vmap(lambda own: jnp.searchsorted(jnp.cumsum(uneven_parts(own, max(3, LEN // 256), LEN, min(2000, LEN // 2), 1)), jnp.arange(LEN), side="right"))(jax.random.split(streams_of[1], SEQS)).reshape((SEQS, LEN)).astype(jnp.int32),
        "norm1_gain": jnp.clip(1.0 + 0.1 * jax.random.normal(streams_of[2], (D,), jnp.float32), 0.5, 1.5).astype(jnp.bfloat16),
        "w_mamba_in": centred(streams_of[3], (D, 2 * MHEADS * MHDIM + 2 * STATE), D ** -0.5, 0.1875, ((0, 32),)),
        "w_delta": centred(streams_of[4], (D, MHEADS), (4 * D) ** -0.5, 0.09375, ((0, 32),)),
        "conv_weight": centred(streams_of[5], (CONVW, MHEADS * MHDIM + 2 * STATE), CONVW ** -0.5, 3.0, ((1, 32),)),
        "conv_bias": centred(streams_of[6], (MHEADS * MHDIM + 2 * STATE,), 0.5, 3.0, ((0, 32),)),
        "delta_bias": jnp.clip(jax.random.uniform(streams_of[7], (MHEADS,), jnp.float32, -6.0, -2.0), -6.0, -2.0).astype(jnp.bfloat16),
        "decay_log": jnp.clip(jax.random.uniform(streams_of[8], (MHEADS,), jnp.float32, -1.0, 1.5), -1.0, 1.5).astype(jnp.bfloat16),
        "skip_gain": jnp.clip(jax.random.uniform(streams_of[9], (MHEADS,), jnp.float32, 0.5, 1.5), 0.5, 1.5).astype(jnp.bfloat16),
        "w_mamba_out": centred(streams_of[10], (MHEADS * MHDIM, D), (MHEADS * MHDIM) ** -0.5, 0.15625, ((0, 32),)),
        "w_qkv": centred(streams_of[11], (D, (AHEADS + 2 * KVHEADS) * AHDIM), D ** -0.5, 0.1875, ((0, 32),)),
        "w_attn_out": centred(streams_of[12], (AHEADS * AHDIM, D), AHDIM ** -0.5, 0.75, ((0, 32),)),
        "norm2_gain": jnp.clip(1.0 + 0.1 * jax.random.normal(streams_of[13], (D,), jnp.float32), 0.5, 1.5).astype(jnp.bfloat16),
        "w_gate_up": centred(streams_of[14], (D, 2 * FF), D ** -0.5, 0.1875, ((0, 32),)),
        "w_down": centred(streams_of[15], (FF, D), FF ** -0.5, 0.125, ((0, 32),)),
        "cotangent": centred(streams_of[16], (SEQS, LEN, D), 1.0, 6.0, ((0, 16), (1, 2))),
    }


EPSILON = 1e-05
ROPE_BASE = 100000000000.0
NEGATIVE = -1e+30

@jax.custom_vjp
def low(v):
    return lax.optimization_barrier(v.astype(jnp.bfloat16)).astype(jnp.float32)

@jax.custom_vjp
def low_back(v):
    return v

def low_keep(v):
    return (low(v), None)

def low_pass(kept, grad):
    return (grad,)

def back_keep(v):
    return (v, None)

def back_low(kept, grad):
    return (low(grad),)
low.defvjp(low_keep, low_pass)
low_back.defvjp(back_keep, back_low)

def matmul(left, right):
    return jnp.dot(left, right, precision=lax.Precision.HIGHEST, preferred_element_type=jnp.float32)

def rms_gain(values, gain):
    scale_inv = lax.rsqrt(lax.optimization_barrier(jnp.mean(values * values, axis=-1, keepdims=True)) + EPSILON)
    return values * scale_inv * gain

def swiglu(joined):
    half_width = joined.shape[-1] // 2
    return jax.nn.silu(joined[:, :half_width]) * joined[:, half_width:]

def tap_masks(seg_padded, first_row, row_count, tap_count):
    own_ids = lax.dynamic_slice_in_dim(seg_padded, first_row + tap_count - 1, row_count)
    listed = []
    for offset in range(tap_count):
        earlier_ids = lax.dynamic_slice_in_dim(seg_padded, first_row + tap_count - 1 - offset, row_count)
        listed.append(earlier_ids == own_ids)
    return jnp.stack(listed).astype(jnp.float32)

def mamba_pre(taps, extended, delta_raw, conv_kernel, conv_shift, delta_bias, decay_log):
    row_count = delta_raw.shape[0]
    tap_count = conv_kernel.shape[0]
    convolved = jnp.zeros((row_count, conv_shift.shape[0]), jnp.float32) + conv_shift[None, :]
    for offset in range(tap_count):
        first_row = tap_count - 1 - offset
        convolved = convolved + conv_kernel[offset][None, :] * extended[first_row:first_row + row_count] * taps[offset][:, None]
    activated = jax.nn.silu(convolved)
    inner_width = MHEADS * MHDIM
    heads_in = activated[:, :inner_width].reshape(row_count, MHEADS, MHDIM)
    b_proj = activated[:, inner_width:inner_width + STATE]
    c_proj = activated[:, inner_width + STATE:]
    step_size = jax.nn.softplus(delta_raw + delta_bias[None, :])
    log_decay = -step_size * jnp.exp(decay_log)[None, :]
    return (heads_in, b_proj, c_proj, step_size, log_decay)

def mamba_state(seg_rows, seg_before, heads_in, b_proj, step_size, log_decay):
    cumulative = jnp.cumsum(log_decay, axis=0)
    final_sum = cumulative[-1]
    carry_gate = jnp.where(seg_rows[-1] == seg_before, jnp.exp(final_sum), 0.0)
    remaining = jnp.where((seg_rows == seg_rows[-1])[:, None], jnp.exp(final_sum[None, :] - cumulative), 0.0) * step_size
    state_part = jnp.einsum('shp,sn->hpn', remaining[:, :, None] * heads_in, b_proj, precision=lax.Precision.HIGHEST)
    return (carry_gate, state_part)

def mamba_out(seg_rows, seg_before, heads_in, b_proj, c_proj, step_size, log_decay, state_in, skip_gain, z_rows):
    row_count = heads_in.shape[0]
    cumulative = jnp.cumsum(log_decay, axis=0)
    places = jnp.arange(row_count, dtype=jnp.int32)
    allowed = ((places[:, None] >= places[None, :]) & (seg_rows[:, None] == seg_rows[None, :]))[:, :, None]
    spread = cumulative[:, None, :] - cumulative[None, :, :]
    decay_map = jnp.where(allowed, jnp.exp(jnp.where(allowed, spread, 0.0)), 0.0)
    cross_terms = jnp.dot(c_proj, b_proj.T, precision=lax.Precision.HIGHEST)
    within = jnp.einsum('tsh,shp->thp', decay_map * cross_terms[:, :, None], step_size[:, :, None] * heads_in, precision=lax.Precision.HIGHEST)
    entering = jnp.where((seg_rows == seg_before)[:, None], jnp.exp(cumulative), 0.0)
    carried = jnp.einsum('tn,hpn->thp', c_proj, state_in, precision=lax.Precision.HIGHEST) * entering[:, :, None]
    summed = within + carried + skip_gain[None, :, None] * heads_in
    return summed.reshape(row_count, MHEADS * MHDIM) * jax.nn.silu(z_rows)

def rope_tables(positions):
    freqs = ROPE_BASE ** (-(jnp.arange(AHDIM // 2).astype(jnp.float32) * 2.0 / AHDIM))
    angles = positions.astype(jnp.float32)[:, None] * freqs[None, :]
    return (jnp.cos(angles)[:, None, :], jnp.sin(angles)[:, None, :])

def rotate_half(values, cosine, sine_vals):
    half_dim = AHDIM // 2
    first_half = values[..., :half_dim]
    second_half = values[..., half_dim:]
    return jnp.concatenate([first_half * cosine - second_half * sine_vals, first_half * sine_vals + second_half * cosine], axis=-1)

def split_heads(cosine, sine_vals, qkv_rows):
    row_count = qkv_rows.shape[0]
    query_width = AHEADS * AHDIM
    key_width = KVHEADS * AHDIM
    queries = qkv_rows[:, :query_width].reshape(row_count, AHEADS, AHDIM)
    keys_rows = qkv_rows[:, query_width:query_width + key_width].reshape(row_count, KVHEADS, AHDIM)
    values_rows = qkv_rows[:, query_width + key_width:].reshape(row_count, KVHEADS, AHDIM)
    return (rotate_half(queries, cosine, sine_vals), rotate_half(keys_rows, cosine, sine_vals), values_rows)

def sequence_forward(rows_in, seg_ids, weights):
    gain_one, mamba_in, delta_proj, conv_kernel, conv_shift, delta_bias, decay_log, skip_gain, mamba_outw, qkv_proj, attn_proj, gain_two, gate_up, down_proj = weights
    seq_length = rows_in.shape[0]
    tap_count = conv_kernel.shape[0]
    inner_width = MHEADS * MHDIM
    normed_one = low(rms_gain(rows_in, gain_one))
    projected = low_back(low(matmul(normed_one, mamba_in)))
    delta_raw = low_back(matmul(normed_one, delta_proj))
    qkv_rows = low_back(matmul(normed_one, qkv_proj))
    z_rows = projected[:, :inner_width]
    conv_in = projected[:, inner_width:]
    extended = jnp.concatenate([jnp.zeros((tap_count - 1, conv_in.shape[1]), jnp.float32), conv_in])
    seg_padded = jnp.concatenate([jnp.full((tap_count - 1,), -1, jnp.int32), seg_ids.astype(jnp.int32)])
    taps = tap_masks(seg_padded, 0, seq_length, tap_count)
    heads_in, b_proj, c_proj, step_size, log_decay = mamba_pre(taps, extended, delta_raw, conv_kernel, conv_shift, delta_bias, decay_log)
    block_total = seq_length // TOK_DEV

    def to_blocks(array):
        return array.reshape((block_total, TOK_DEV) + array.shape[1:])
    before_ids = seg_padded[tap_count - 2:tap_count - 2 + seq_length].reshape(block_total, TOK_DEV)[:, 0]

    def ssd_step(state_in, block):
        heads_b, b_blk, c_blk, step_blk, decay_blk, z_blk, seg_blk, before_blk = block
        carry_gate, state_part = mamba_state(seg_blk, before_blk, heads_b, b_blk, step_blk, decay_blk)
        mixed_blk = mamba_out(seg_blk, before_blk, heads_b, b_blk, c_blk, step_blk, decay_blk, state_in, skip_gain, z_blk)
        return (carry_gate[:, None, None] * state_in + state_part, mixed_blk)
    start_state = jnp.zeros((MHEADS, MHDIM, STATE), jnp.float32)
    _, mixed_blocks = lax.scan(jax.checkpoint(ssd_step), start_state, (to_blocks(heads_in), to_blocks(b_proj), to_blocks(c_proj), to_blocks(step_size), to_blocks(log_decay), to_blocks(z_rows), to_blocks(seg_ids), before_ids))
    mixed_low = low(mixed_blocks.reshape(seq_length, inner_width))
    mixer = low_back(matmul(mixed_low, mamba_outw))
    positions = jnp.arange(seq_length, dtype=jnp.int32)
    cosine, sine_vals = rope_tables(positions)
    queries, keys_rows, values_rows = split_heads(cosine, sine_vals, qkv_rows)
    queries = low(queries)
    keys_rows = low(keys_rows)
    values_rows = low(values_rows)
    group_size = AHEADS // KVHEADS
    block_len = min(512, seq_length)
    query_blocks = seq_length // block_len
    query_groups = queries.reshape(query_blocks, block_len, KVHEADS, group_size, AHDIM)

    def attend(block):
        query_blk, pos_blk, seg_blk = block
        raw_scores = jnp.einsum('tgid,kgd->gitk', query_blk, keys_rows, precision=lax.Precision.HIGHEST) * AHDIM ** (-0.5)
        raw_scores = low_back(raw_scores)
        allowed = (positions[None, :] <= pos_blk[:, None]) & (seg_ids[None, :] == seg_blk[:, None])
        scores = jnp.where(allowed[None, None], raw_scores, NEGATIVE)
        probs = low(jax.nn.softmax(scores, axis=-1))
        return jnp.einsum('gitk,kgd->tgid', probs, values_rows, precision=lax.Precision.HIGHEST)
    attended = lax.map(jax.checkpoint(attend), (query_groups, positions.reshape(query_blocks, block_len), seg_ids.reshape(query_blocks, block_len)))
    attended = low_back(low(attended.reshape(seq_length, AHEADS * AHDIM)))
    attn_rows = low_back(matmul(attended, attn_proj))
    residual = rows_in + mixer + attn_rows
    normed_two = low(rms_gain(residual, gain_two))
    gate_rows = low_back(matmul(normed_two, gate_up))
    hidden = low(swiglu(gate_rows))
    return residual + low_back(matmul(hidden, down_proj))

def reference(tokens, segment_ids, norm1_gain, w_mamba_in, w_delta, conv_weight, conv_bias, delta_bias, decay_log, skip_gain, w_mamba_out, w_qkv, w_attn_out, norm2_gain, w_gate_up, w_down, cotangent):
    weights = tuple((item.astype(jnp.float32) for item in (norm1_gain, w_mamba_in, w_delta, conv_weight, conv_bias, delta_bias, decay_log, skip_gain, w_mamba_out, w_qkv, w_attn_out, norm2_gain, w_gate_up, w_down)))
    inputs = tokens.astype(jnp.float32)

    def forward(inputs, weights):

        def one_sequence(pair):
            return sequence_forward(pair[0], pair[1], weights)
        return lax.map(jax.checkpoint(one_sequence), (inputs, segment_ids))
    outputs, backward = jax.vjp(forward, inputs, weights)
    grad_inputs, grads = backward(cotangent.astype(jnp.float32))
    return (outputs.astype(jnp.bfloat16), grad_inputs, grads[0], grads[1], grads[2], grads[3], grads[4], grads[5], grads[6], grads[7], grads[8], grads[9], grads[10], grads[11], grads[12], grads[13])
```

```python
import math
from functools import partial

import jax
import jax.numpy as jnp
from jax import lax
from jax.experimental import pallas as pl
from jax.experimental.pallas import tpu as pltpu
from jax.sharding import PartitionSpec as P

MHEADS = 24
MHDIM = 64
STATE = 128
AHEADS = 8
KVHEADS = 2
AHDIM = 64

INNER = MHEADS * MHDIM
CONVD = INNER + 2 * STATE
QWIDTH = AHEADS * AHDIM
KWIDTH = KVHEADS * AHDIM
GROUPS = 3
GHEADS = MHEADS // GROUPS
GLANES = GHEADS * MHDIM
STRIP = 128

EPSILON = 1e-05
ROPE_BASE = 100000000000.0
NEGATIVE = -1e30
LOG2E = math.log2(math.e)

F32 = jnp.float32
BF16 = jnp.bfloat16


def dot_nn(a, b):
    return lax.dot_general(a, b, (((1,), (0,)), ((), ())), preferred_element_type=F32)


def dot_nt(a, b):
    return lax.dot_general(a, b, (((1,), (1,)), ((), ())), preferred_element_type=F32)


def dot_tn(a, b):
    return lax.dot_general(a, b, (((0,), (0,)), ((), ())), preferred_element_type=F32)


def mesh_bits():
    bits = []
    for axis in ("dp", "seq"):
        size = lax.axis_size(axis)
        level = size // 2
        while level:
            bits.append((axis, level))
            level //= 2
    return bits


def bit_orders():
    bits = mesh_bits()
    seq = [b for b in bits if b[0] == "seq"][::-1]
    dp = [b for b in bits if b[0] == "dp"][::-1]
    pair, second, rest = dp[:1], dp[1:2], dp[2:]
    return (
        pair + seq + second + rest,
        pair + second + rest + seq,
        pair + rest + seq + second,
    )


def swap(value, bit):
    axis, level = bit
    size = lax.axis_size(axis)
    return lax.ppermute(value, axis, [(i, i ^ level) for i in range(size)])


def bit_here(bit):
    axis, level = bit
    return (lax.axis_index(axis) // level) % 2


def halve(full, order):
    left = mesh_bits()
    total = full.shape[0]
    rows = total >> len(left)
    value = full.reshape((2,) * len(left) + (rows, full.shape[1]))
    for bit in order:
        place = left.index(bit)
        here = bit_here(bit)
        out = lax.dynamic_index_in_dim(value, 1 - here, place, keepdims=False)
        kept = lax.dynamic_index_in_dim(value, here, place, keepdims=False)
        got = swap(out, bit)
        left.remove(bit)
        value = kept.astype(F32) + got.astype(F32)
        if left:
            value = value.astype(BF16)
    return value


def double(shard, order):
    bits = mesh_bits()
    held = []
    value = shard
    for bit in reversed(order):
        got = swap(value, bit)
        here = bit_here(bit)
        held = [b for b in bits if b in held or b == bit]
        place = held.index(bit)
        low = jnp.where(here == 0, value, got)
        high = jnp.where(here == 0, got, value)
        value = jnp.stack([low, high], axis=place)
    return value.reshape((shard.shape[0] << len(bits), shard.shape[1]))


def total_everywhere(value):
    for bit in mesh_bits():
        value = value + swap(value, bit)
    return value


def compose_maps(earlier, later):
    return (later[0] * earlier[0], later[0][None, :] * earlier[1] + later[1])


def state_from_behind(gate, part):
    count = lax.axis_size("seq")
    low = part.astype(BF16)
    if count == 2:
        return lax.ppermute(low, "seq", [(0, 1)]).astype(F32)
    gates = lax.all_gather(gate.astype(BF16), "seq")
    parts = lax.all_gather(low, "seq")
    start = (jnp.ones_like(gate), jnp.zeros_like(part))

    def one(step, state):
        return compose_maps(
            state,
            (
                lax.dynamic_index_in_dim(gates, step, 0, False).astype(F32),
                lax.dynamic_index_in_dim(parts, step, 0, False).astype(F32),
            ),
        )

    return lax.fori_loop(0, lax.axis_index("seq"), one, start)[1]


def state_from_ahead(gate, part):
    count = lax.axis_size("seq")
    low = part.astype(BF16)
    if count == 2:
        return lax.ppermute(low, "seq", [(1, 0)]).astype(F32)
    gates = lax.all_gather(gate.astype(BF16), "seq")
    parts = lax.all_gather(low, "seq")
    start = (jnp.ones_like(gate), jnp.zeros_like(part))
    place = lax.axis_index("seq")

    def one(step, state):
        at = count - 1 - step
        return compose_maps(
            state,
            (
                lax.dynamic_index_in_dim(gates, at, 0, False).astype(F32),
                lax.dynamic_index_in_dim(parts, at, 0, False).astype(F32),
            ),
        )

    return lax.fori_loop(0, count - 1 - place, one, start)[1]


def neighbour(value, steps):
    count = lax.axis_size("seq")
    first, last = (max(0, -steps), min(count, count - steps))
    return lax.ppermute(value, "seq", [(s, s + steps) for s in range(first, last)])


PARAMS = pltpu.CompilerParams(vmem_limit_bytes=48 * 1024 * 1024)


def lane_is_low(rows):
    return lax.broadcasted_iota(jnp.int32, (rows, 128), 1) < MHDIM


def spread(low, vec, head):
    return jnp.where(low, vec[:, head : head + 1], vec[:, head + 1 : head + 2])


def ssd_forward_kernel(x_ref, b_ref, c_ref, vec_ref, row_ref, segc_ref, segr_ref, y_ref, st_ref, cb_ref):
    length = x_ref.shape[0]

    @pl.when(pl.program_id(0) == 0)
    def _():
        t = lax.broadcasted_iota(jnp.int32, (length, length), 0)
        s = lax.broadcasted_iota(jnp.int32, (length, length), 1)
        seen = (t >= s) & (segc_ref[...] == segr_ref[...])
        cb = dot_nt(c_ref[...].astype(BF16), b_ref[...].astype(BF16))
        cb_ref[...] = jnp.where(seen, cb, 0.0)

    b_low = b_ref[...].astype(BF16)
    wide = lane_is_low(length)
    narrow = lane_is_low(STRIP)
    dt = vec_ref[0, :, 0:GHEADS]
    rem = vec_ref[0, :, 2 * GHEADS : 3 * GHEADS]
    for pair in range(GHEADS // 2):
        lanes = slice(pair * 128, (pair + 1) * 128)
        xd = x_ref[:, lanes] * spread(wide, dt, 2 * pair)
        xd_low = xd.astype(BF16)
        st_ref[:, lanes] = dot_tn(b_low, (xd * spread(wide, rem, 2 * pair)).astype(BF16))
        for strip in range(length // STRIP):
            first, width = strip * STRIP, (strip + 1) * STRIP
            halves = []
            for head in (2 * pair, 2 * pair + 1):
                at = GHEADS + head
                gap = vec_ref[0, first : first + STRIP, at : at + 1] - row_ref[head : head + 1, :width]
                decay = jnp.exp2(jnp.minimum(gap, 0.0))
                m = (decay * cb_ref[first : first + STRIP, :width]).astype(BF16)
                halves.append(dot_nn(m, xd_low[:width]))
            y_ref[first : first + STRIP, lanes] = jnp.where(narrow, halves[0], halves[1])


def group_specs(length):
    x_spec = pl.BlockSpec((length, GLANES), lambda g: (0, g))
    s_spec = pl.BlockSpec((STATE, GLANES), lambda g: (0, g))
    n_spec = pl.BlockSpec((length, STATE), lambda g: (0, 0))
    v_spec = pl.BlockSpec((1, length, 4 * GHEADS), lambda g: (g, 0, 0))
    r_spec = pl.BlockSpec((GHEADS, length), lambda g: (g, 0))
    return x_spec, s_spec, n_spec, v_spec, r_spec


def ssd_forward(x, b, c, vec, row, seg_col, seg_row):
    length = x.shape[0]
    x_spec, s_spec, n_spec, v_spec, r_spec = group_specs(length)
    return pl.pallas_call(
        ssd_forward_kernel,
        grid=(GROUPS,),
        in_specs=[
            x_spec, n_spec, n_spec, v_spec, r_spec,
            pl.BlockSpec((length, 1), lambda g: (0, 0)),
            pl.BlockSpec((1, length), lambda g: (0, 0)),
        ],
        out_specs=[x_spec, s_spec],
        out_shape=[
            jax.ShapeDtypeStruct((length, INNER), F32),
            jax.ShapeDtypeStruct((STATE, INNER), F32),
        ],
        scratch_shapes=[pltpu.VMEM((length, length), F32)],
        compiler_params=PARAMS,
        name="ssd_forward",
    )(x, b, c, vec, row, seg_col, seg_row)


def silu_parts(v):
    sig = 1.0 / (1.0 + jnp.exp(-v))
    return v * sig, sig * (1.0 + v * (1.0 - sig))


def ssd_finish_kernel(y0_ref, x_ref, z_ref, c_ref, st_ref, vec_ref, skip_ref, y_ref, ym_ref):
    length = x_ref.shape[0]
    wide = lane_is_low(length)
    ent = vec_ref[0, :, 3 * GHEADS : 4 * GHEADS]
    c_low = c_ref[...].astype(BF16)
    for pair in range(GHEADS // 2):
        lanes = slice(pair * 128, (pair + 1) * 128)
        cs = dot_nn(c_low, st_ref[:, lanes].astype(BF16))
        y = y0_ref[:, lanes] + spread(wide, ent, 2 * pair) * cs + skip_ref[:, lanes] * x_ref[:, lanes]
        gate, _ = silu_parts(z_ref[:, lanes].astype(F32))
        y_ref[:, lanes] = y
        ym_ref[:, lanes] = (y * gate).astype(BF16)


def ssd_finish(y0, x, z, c, state, vec, skip):
    length = x.shape[0]
    x_spec, s_spec, n_spec, v_spec, _ = group_specs(length)
    return pl.pallas_call(
        ssd_finish_kernel,
        grid=(GROUPS,),
        in_specs=[x_spec, x_spec, x_spec, n_spec, s_spec, v_spec, pl.BlockSpec((1, GLANES), lambda g: (0, g))],
        out_specs=[x_spec, x_spec],
        out_shape=[
            jax.ShapeDtypeStruct((length, INNER), F32),
            jax.ShapeDtypeStruct((length, INNER), BF16),
        ],
        compiler_params=PARAMS,
        name="ssd_finish",
    )(y0, x, z, c, state, vec, skip)


def ssd_gate_kernel(dym_ref, y_ref, x_ref, z_ref, c_ref, vec_ref, dy_ref, dz_ref, ds_ref, skip_ref):
    length = x_ref.shape[0]
    wide = lane_is_low(length)
    ent = vec_ref[0, :, 3 * GHEADS : 4 * GHEADS]
    c_low = c_ref[...].astype(BF16)
    for pair in range(GHEADS // 2):
        lanes = slice(pair * 128, (pair + 1) * 128)
        gate, slope = silu_parts(z_ref[:, lanes].astype(F32))
        dym = dym_ref[:, lanes]
        dy = dym * gate
        dy_ref[:, lanes] = dy
        dz_ref[:, lanes] = (dym * y_ref[:, lanes] * slope).astype(BF16)
        ds_ref[:, lanes] = dot_tn(c_low, (dy * spread(wide, ent, 2 * pair)).astype(BF16))
        skip_ref[:, lanes] = jnp.sum(dy * x_ref[:, lanes], axis=0, keepdims=True)


def ssd_gate(dym, y, x, z, c, vec):
    length = x.shape[0]
    x_spec, s_spec, n_spec, v_spec, _ = group_specs(length)
    one_spec = pl.BlockSpec((1, GLANES), lambda g: (0, g))
    return pl.pallas_call(
        ssd_gate_kernel,
        grid=(GROUPS,),
        in_specs=[x_spec, x_spec, x_spec, x_spec, n_spec, v_spec],
        out_specs=[x_spec, x_spec, s_spec, one_spec],
        out_shape=[
            jax.ShapeDtypeStruct((length, INNER), F32),
            jax.ShapeDtypeStruct((length, INNER), BF16),
            jax.ShapeDtypeStruct((STATE, INNER), F32),
            jax.ShapeDtypeStruct((1, INNER), F32),
        ],
        compiler_params=PARAMS,
        name="ssd_gate",
    )(dym, y, x, z, c, vec)


def ssd_backward_kernel(
    x_ref, dy_ref, b_ref, c_ref, st_ref, dst_ref, vec_ref, row_ref, segc_ref, segr_ref, skip_ref,
    dx_ref, db_ref, dc_ref, cols_ref, rows_ref, bc_ref, dbc_ref, xd_ref, sum_ref,
):
    length = x_ref.shape[0]
    group = pl.program_id(0)

    @pl.when(group == 0)
    def _():
        s = lax.broadcasted_iota(jnp.int32, (length, length), 0)
        t = lax.broadcasted_iota(jnp.int32, (length, length), 1)
        seen = (t >= s) & (segc_ref[...] == segr_ref[...])
        bc = dot_nt(b_ref[...].astype(BF16), c_ref[...].astype(BF16))
        bc_ref[...] = jnp.where(seen, bc, 0.0)
        dbc_ref[...] = jnp.zeros_like(dbc_ref)
        db_ref[...] = jnp.zeros_like(db_ref)
        dc_ref[...] = jnp.zeros_like(dc_ref)
        cols_ref[...] = jnp.zeros_like(cols_ref)

    b_low = b_ref[...].astype(BF16)
    c_low = c_ref[...].astype(BF16)
    wide = lane_is_low(length)
    narrow = lane_is_low(STRIP)
    lane = lax.broadcasted_iota(jnp.int32, (STRIP, 128), 1)
    spot = lax.broadcasted_iota(jnp.int32, (128, 128), 0) // MHDIM
    place = lax.broadcasted_iota(jnp.int32, (128, 128), 1)
    dt = vec_ref[0, :, 0:GHEADS]
    rem = vec_ref[0, :, 2 * GHEADS : 3 * GHEADS]
    ent = vec_ref[0, :, 3 * GHEADS : 4 * GHEADS]
    rows_ref[...] = jnp.zeros_like(rows_ref)
    for pair in range(GHEADS // 2):
        lanes = slice(pair * 128, (pair + 1) * 128)
        x = x_ref[:, lanes]
        dy = dy_ref[:, lanes]
        dtx = spread(wide, dt, 2 * pair)
        remx = spread(wide, rem, 2 * pair)
        entx = spread(wide, ent, 2 * pair)
        dy_low = dy.astype(BF16)
        xd_ref[...] = (x * dtx).astype(BF16)
        st_low = st_ref[:, lanes].astype(BF16)
        dst_low = dst_ref[:, lanes].astype(BF16)
        carried = remx * dot_nn(b_low, dst_low)
        entered = entx * dot_nn(c_low, st_low)
        dc_ref[...] += dot_nt((entx * dy).astype(BF16), st_low)
        db_ref[...] += dot_nt((dtx * remx * x).astype(BF16), dst_low)
        for strip in range(length // STRIP):
            first = strip * STRIP
            xd = xd_ref[first : first + STRIP, :]
            dys = dy_low[first:]
            halves = []
            for half in range(2):
                head = 2 * pair + half
                mine = narrow if half == 0 else ~narrow
                gap = row_ref[head : head + 1, first:] - vec_ref[0, first : first + STRIP, GHEADS + head : GHEADS + head + 1]
                decay = jnp.exp2(jnp.minimum(gap, 0.0))
                bc = bc_ref[first : first + STRIP, first:]
                m = (decay * bc).astype(BF16)
                halves.append(dot_nn(m, dys))
                dg = decay * dot_nt(jnp.where(mine, xd, jnp.zeros_like(xd)), dys)
                dbc_ref[first : first + STRIP, first:] += dg
                e = dg * bc
                rows_ref[head : head + 1, first:] += jnp.sum(e, axis=0, keepdims=True)
                gone = jnp.sum(e, axis=1, keepdims=True)
                at = group * GHEADS + head
                cols_ref[3, first : first + STRIP, :] += jnp.where(lane == at, gone, 0.0)
            dxd = jnp.where(narrow, halves[0], halves[1]) + carried[first : first + STRIP]
            sum_ref[first : first + STRIP, :] = dxd
        dxd = sum_ref[...]
        dx_ref[:, lanes] = dtx * dxd + skip_ref[:, lanes] * dy
        pick = (place == group * GHEADS + 2 * pair + spot).astype(BF16)

        def per_head(value):
            high = value.astype(BF16)
            rest = (value - high.astype(F32)).astype(BF16)
            return dot_nn(high, pick) + dot_nn(rest, pick)

        cols_ref[0] += per_head(dxd * x)
        cols_ref[1] += per_head(dtx * x * carried)
        cols_ref[2] += per_head(dy * entered)

    @pl.when(group == GROUPS - 1)
    def _():
        s = lax.broadcasted_iota(jnp.int32, (length, length), 0)
        t = lax.broadcasted_iota(jnp.int32, (length, length), 1)
        seen = (t >= s) & (segc_ref[...] == segr_ref[...])
        dbc = jnp.where(seen, dbc_ref[...], 0.0).astype(BF16)
        db_ref[...] += dot_nn(dbc, c_low)
        dc_ref[...] += dot_tn(dbc, b_low)


def ssd_backward(x, dy, b, c, state, dstate, vec, row, seg_col, seg_row, skip):
    length = x.shape[0]
    x_spec, s_spec, n_spec, v_spec, r_spec = group_specs(length)
    return pl.pallas_call(
        ssd_backward_kernel,
        grid=(GROUPS,),
        in_specs=[
            x_spec, x_spec, n_spec, n_spec, s_spec, s_spec, v_spec, r_spec,
            pl.BlockSpec((length, 1), lambda g: (0, 0)),
            pl.BlockSpec((1, length), lambda g: (0, 0)),
            pl.BlockSpec((1, GLANES), lambda g: (0, g)),
        ],
        out_specs=[x_spec, n_spec, n_spec, pl.BlockSpec((4, length, 128), lambda g: (0, 0, 0)), r_spec],
        out_shape=[
            jax.ShapeDtypeStruct((length, INNER), F32),
            jax.ShapeDtypeStruct((length, STATE), F32),
            jax.ShapeDtypeStruct((length, STATE), F32),
            jax.ShapeDtypeStruct((4, length, 128), F32),
            jax.ShapeDtypeStruct((MHEADS, length), F32),
        ],
        scratch_shapes=[
            pltpu.VMEM((length, length), F32),
            pltpu.VMEM((length, length), F32),
            pltpu.VMEM((length, 128), BF16),
            pltpu.VMEM((length, 128), F32),
        ],
        compiler_params=PARAMS,
        name="ssd_backward",
    )(x, dy, b, c, state, dstate, vec, row, seg_col, seg_row, skip)


def turn(value, cosine, sine):
    low = (lax.broadcasted_iota(jnp.int32, value.shape, 1) % AHDIM) < AHDIM // 2
    other = jnp.where(low, pltpu.roll(value, 128 - AHDIM // 2, 1), pltpu.roll(value, AHDIM // 2, 1))
    return value * cosine + other * sine


def rope_kernel(qkv_ref, cos_ref, sin_ref, q_ref, kv_ref):
    cosine, sine = cos_ref[...], sin_ref[...]
    scale = AHDIM ** (-0.5)
    for at in range(QWIDTH // 128):
        lanes = slice(at * 128, (at + 1) * 128)
        q_ref[:, lanes] = (turn(qkv_ref[:, lanes], cosine, sine).astype(BF16).astype(F32) * scale).astype(BF16)
    kv_ref[:, :KWIDTH] = turn(qkv_ref[:, QWIDTH : QWIDTH + KWIDTH], cosine, sine).astype(BF16)
    kv_ref[:, KWIDTH:] = qkv_ref[:, QWIDTH + KWIDTH :].astype(BF16)


def rope(qkv, cosine, sine):
    length = qkv.shape[0]
    return pl.pallas_call(
        rope_kernel,
        out_shape=[
            jax.ShapeDtypeStruct((length, QWIDTH), BF16),
            jax.ShapeDtypeStruct((length, 2 * KWIDTH), BF16),
        ],
        compiler_params=PARAMS,
        name="rope",
    )(qkv, cosine, sine)


def unrope_kernel(dq_ref, dkv_ref, more_ref, cos_ref, sin_ref, out_ref):
    cosine, sine = cos_ref[...], -sin_ref[...]
    scale = AHDIM ** (-0.5)
    for at in range(QWIDTH // 128):
        lanes = slice(at * 128, (at + 1) * 128)
        out_ref[:, lanes] = (turn(dq_ref[:, lanes], cosine, sine) * scale).astype(BF16)
    dkv = dkv_ref[...] + more_ref[...].astype(F32)
    out_ref[:, QWIDTH : QWIDTH + KWIDTH] = turn(dkv[:, :KWIDTH], cosine, sine).astype(BF16)
    out_ref[:, QWIDTH + KWIDTH :] = dkv[:, KWIDTH:].astype(BF16)


def unrope(dq, dkv, more, cosine, sine):
    length = dq.shape[0]
    return pl.pallas_call(
        unrope_kernel,
        out_shape=jax.ShapeDtypeStruct((length, QWIDTH + 2 * KWIDTH), BF16),
        compiler_params=PARAMS,
        name="unrope",
    )(dq, dkv, more, cosine, sine)


def attend_kernel(rank_ref, q_ref, k_ref, v_ref, segq_ref, segk_ref, o_ref, lse_ref, top_ref, sum_ref, acc_ref, mask_ref):
    length = q_ref.shape[0]
    rank = rank_ref[0]
    top_ref[...] = jnp.full_like(top_ref, NEGATIVE)
    sum_ref[...] = jnp.zeros_like(sum_ref)
    acc_ref[...] = jnp.zeros_like(acc_ref)
    narrow = lane_is_low(STRIP)

    def block(step, carry):
        at = rank - step
        t = lax.broadcasted_iota(jnp.int32, (length, length), 0) + rank * length
        s = lax.broadcasted_iota(jnp.int32, (length, length), 1) + at * length
        seen = (s <= t) & (segq_ref[...] == segk_ref[pl.ds(at, 1), :])
        mask_ref[...] = jnp.where(seen, 0.0, NEGATIVE)
        start = pl.multiple_of(at * length, length)
        for head in range(AHEADS):
            kv_head = head // (AHEADS // KVHEADS)
            mine = narrow if head % 2 == 0 else ~narrow
            lanes = slice(head // 2 * 128, (head // 2 + 1) * 128)
            keys = k_ref[kv_head, pl.ds(start, length), :]
            values = v_ref[kv_head, pl.ds(start, length), :]
            for strip in range(length // STRIP):
                rows = slice(strip * STRIP, (strip + 1) * STRIP)
                q = q_ref[rows, lanes]
                scores = dot_nt(jnp.where(mine, q, jnp.zeros_like(q)), keys) + mask_ref[rows, :]
                old = top_ref[head, rows, :]
                new = jnp.maximum(old, jnp.max(scores, axis=1, keepdims=True))
                fade = jnp.exp(old - new)
                probs = jnp.exp(scores - new[:, :1])
                sum_ref[head, rows, :] = sum_ref[head, rows, :] * fade + jnp.sum(probs, axis=1, keepdims=True)
                top_ref[head, rows, :] = new
                acc = acc_ref[rows, lanes]
                acc_ref[rows, lanes] = jnp.where(mine, acc * fade + dot_nn(probs.astype(BF16), values), acc)
        return carry

    lax.fori_loop(0, rank + 1, block, 0)
    lane = lax.broadcasted_iota(jnp.int32, (length, 128), 1)
    stats = jnp.zeros((length, 128), F32)
    low = lane_is_low(length)
    for pair in range(AHEADS // 2):
        lanes = slice(pair * 128, (pair + 1) * 128)
        o_ref[:, lanes] = acc_ref[:, lanes] / jnp.where(low, sum_ref[2 * pair], sum_ref[2 * pair + 1])
    for head in range(AHEADS):
        stats = jnp.where(lane == head, top_ref[head] + jnp.log(sum_ref[head]), stats)
    lse_ref[...] = stats


def attend(rank, q, keys, values, seg_col, seg_blocks):
    length = q.shape[0]
    vmem = pl.BlockSpec(memory_space=pltpu.VMEM)
    return pl.pallas_call(
        attend_kernel,
        in_specs=[pl.BlockSpec(memory_space=pltpu.SMEM)] + [vmem] * 5,
        out_specs=[vmem, vmem],
        out_shape=[
            jax.ShapeDtypeStruct((length, QWIDTH), F32),
            jax.ShapeDtypeStruct((length, 128), F32),
        ],
        scratch_shapes=[
            pltpu.VMEM((AHEADS, length, 128), F32),
            pltpu.VMEM((AHEADS, length, 128), F32),
            pltpu.VMEM((length, QWIDTH), F32),
            pltpu.VMEM((length, length), F32),
        ],
        compiler_params=PARAMS,
        name="attend",
    )(rank, q, keys, values, seg_col, seg_blocks)


def attend_backward_kernel(
    rank_ref, q_ref, k_ref, v_ref, do_ref, lse_ref, delta_ref, segq_ref, segk_ref, dq_ref, dkv_ref
):
    length = q_ref.shape[0]
    total = k_ref.shape[1]
    rank = rank_ref[0]
    dq_ref[...] = jnp.zeros_like(dq_ref)
    dkv_ref[...] = jnp.zeros_like(dkv_ref)
    narrow = lane_is_low(STRIP)
    per = AHEADS // KVHEADS

    def strip_of(step, carry):
        start = pl.multiple_of(step * STRIP, STRIP)
        s = lax.broadcasted_iota(jnp.int32, (STRIP, length), 0) + start
        t = lax.broadcasted_iota(jnp.int32, (STRIP, length), 1) + rank * length
        seen = (s <= t) & (segk_ref[pl.ds(start, STRIP), :] == segq_ref[...])
        mask = jnp.where(seen, 0.0, NEGATIVE)
        sums = []
        for kv_head in range(KVHEADS):
            keys = k_ref[kv_head, pl.ds(start, STRIP), :]
            values = v_ref[kv_head, pl.ds(start, STRIP), :]
            dk = jnp.zeros((STRIP, 128), F32)
            dv = jnp.zeros((STRIP, 128), F32)
            for head in range(kv_head * per, (kv_head + 1) * per):
                mine = narrow if head % 2 == 0 else ~narrow
                lanes = slice(head // 2 * 128, (head // 2 + 1) * 128)
                q = q_ref[:, lanes]
                do = do_ref[:, lanes]
                own_keys = jnp.where(mine, keys, jnp.zeros_like(keys))
                own_values = jnp.where(mine, values, jnp.zeros_like(values))
                probs = jnp.exp(dot_nt(own_keys, q) + mask - lse_ref[head : head + 1, :])
                dp = dot_nt(own_values, do)
                ds = (probs * (dp - delta_ref[head : head + 1, :])).astype(BF16)
                dv += jnp.where(mine, dot_nn(probs.astype(BF16), do), 0.0)
                dk += jnp.where(mine, dot_nn(ds, q), 0.0)
                dq_ref[:, lanes] += dot_tn(ds, own_keys)
            sums.append((dk + pltpu.roll(dk, AHDIM, 1), dv + pltpu.roll(dv, AHDIM, 1)))
        dkv_ref[pl.ds(start, STRIP), :KWIDTH] = jnp.where(narrow, sums[0][0], sums[1][0])
        dkv_ref[pl.ds(start, STRIP), KWIDTH:] = jnp.where(narrow, sums[0][1], sums[1][1])
        return carry

    lax.fori_loop(0, (rank + 1) * (length // STRIP), strip_of, 0)


def attend_backward(rank, q, keys, values, do, lse, delta, seg_row, seg_keys):
    length, total = q.shape[0], keys.shape[1]
    vmem = pl.BlockSpec(memory_space=pltpu.VMEM)
    return pl.pallas_call(
        attend_backward_kernel,
        in_specs=[pl.BlockSpec(memory_space=pltpu.SMEM)] + [vmem] * 8,
        out_specs=[vmem, vmem],
        out_shape=[
            jax.ShapeDtypeStruct((length, QWIDTH), F32),
            jax.ShapeDtypeStruct((total, 2 * KWIDTH), F32),
        ],
        compiler_params=PARAMS,
        name="attend_backward",
    )(rank, q, keys, values, do, lse, delta, seg_row, seg_keys)


def gather_keyvals(own):
    count = lax.axis_size("seq")
    if count == 2:
        got = lax.ppermute(own, "seq", [(0, 1)])
        first = lax.axis_index("seq") == 0
        return jnp.concatenate([jnp.where(first, own, got), own])
    return lax.all_gather(own, "seq", axis=0, tiled=True)


def scatter_keyval_grads(grads, length):
    count = lax.axis_size("seq")
    place = lax.axis_index("seq")
    if count == 2:
        own = lax.dynamic_slice_in_dim(grads, place * length, length)
        return own, lax.ppermute(grads[:length].astype(BF16), "seq", [(1, 0)])
    total = lax.psum_scatter(grads.astype(BF16), "seq", scatter_dimension=0, tiled=True)
    return jnp.zeros((length, grads.shape[1]), F32), total


def fit(value, rows):
    flat = value.reshape(-1)
    columns = -(-flat.shape[0] // rows)
    return jnp.pad(flat, (0, rows * columns - flat.shape[0])).reshape(rows, columns)


def on_device(
    tokens,
    segment_ids,
    norm1_gain,
    w_mamba_in,
    w_delta,
    conv_weight,
    conv_bias,
    delta_bias,
    decay_log,
    skip_gain,
    w_mamba_out,
    w_qkv,
    w_attn_out,
    norm2_gain,
    w_gate_up,
    w_down,
    cotangent,
):
    order_x, order_y, order_z = bit_orders()
    count = lax.axis_size("dp") * lax.axis_size("seq")
    rows = w_qkv.shape[0]
    width = rows * count
    taps_count, channels = conv_weight.shape
    conv_cols = -(-taps_count * channels // rows)
    bias_cols = -(-channels // rows)
    small = jnp.concatenate(
        [w_delta, norm1_gain[:, None], norm2_gain[:, None], fit(conv_weight, rows), fit(conv_bias, rows)], axis=1
    )
    small_width = 128 * (-(-small.shape[1] // 128))
    small = jnp.pad(small, ((0, 0), (0, small_width - small.shape[1])))

    gate_up = lax.all_gather(w_gate_up, ("dp", "seq"), axis=0, tiled=True)
    down = lax.all_gather(w_down, ("dp", "seq"), axis=0, tiled=True)
    w_q = double(jnp.concatenate([w_qkv, small], axis=1), order_z)
    w_x = double(w_mamba_in[:, INNER:], order_x)
    w_z = double(w_mamba_in[:, :INNER], order_y)
    w_mo = double(w_mamba_out, order_x)
    w_ao = double(w_attn_out, order_y)

    smalls = w_q[:, QWIDTH + 2 * KWIDTH :]
    gain_one = smalls[:, MHEADS].astype(F32)
    gain_two = smalls[:, MHEADS + 1].astype(F32)
    at = MHEADS + 2
    conv_kernel = smalls[:, at : at + conv_cols].reshape(count, rows * conv_cols)[:, : taps_count * channels]
    conv_kernel = conv_kernel.reshape(count, taps_count, channels).transpose(1, 0, 2)
    conv_kernel = conv_kernel.reshape(taps_count, count * channels).astype(F32)
    at += conv_cols
    conv_shift = smalls[:, at : at + bias_cols].reshape(count, rows * bias_cols)[:, :channels]
    conv_shift = conv_shift.reshape(count * channels).astype(F32)

    length = tokens.shape[1]
    seg_full = segment_ids[0]
    total = seg_full.shape[0]
    rank = lax.axis_index("seq")
    first_row = rank * length
    back = taps_count - 1
    seg_padded = jnp.concatenate([jnp.full((back,), -1, jnp.int32), seg_full])
    seg_own = lax.dynamic_slice_in_dim(seg_full, first_row, length)
    seg_before = lax.dynamic_slice_in_dim(seg_padded, first_row + back - 1, 1)[0]
    taps = [
        (lax.dynamic_slice_in_dim(seg_padded, first_row + back - j, length) == seg_own).astype(F32)[:, None]
        for j in range(taps_count)
    ]
    seg_col = seg_own[:, None]
    seg_row = seg_own[None, :]
    rank_arg = rank.astype(jnp.int32).reshape(1)

    inputs = tokens[0].astype(F32)
    r1 = lax.rsqrt(jnp.mean(inputs * inputs, axis=-1, keepdims=True) + EPSILON)
    n1 = (inputs * r1 * gain_one[None, :]).astype(BF16)
    qkv_small = dot_nn(n1, w_q)
    qkv = qkv_small[:, : QWIDTH + 2 * KWIDTH]
    delta_raw = qkv_small[:, QWIDTH + 2 * KWIDTH : QWIDTH + 2 * KWIDTH + MHEADS]
    xbc = dot_nn(n1, w_x).astype(BF16)
    z = dot_nn(n1, w_z).astype(BF16)

    freqs = ROPE_BASE ** (-(jnp.arange(AHDIM // 2).astype(F32) * 2.0 / AHDIM))
    angles = (first_row + jnp.arange(length, dtype=jnp.int32)).astype(F32)[:, None] * freqs[None, :]
    cosine = jnp.tile(jnp.cos(angles), (1, 4))
    sine_half = jnp.sin(angles)
    sine = jnp.tile(jnp.concatenate([-sine_half, sine_half], axis=1), (1, 2))
    q, keyvals = rope(qkv, cosine, sine)
    all_keyvals = gather_keyvals(keyvals)

    def doubled(start):
        return jnp.stack(
            [
                jnp.tile(all_keyvals[:, start + i * AHDIM : start + (i + 1) * AHDIM], (1, 2))
                for i in range(KVHEADS)
            ]
        )

    keys, values = doubled(0), doubled(KWIDTH)

    halo = neighbour(xbc[length - back :], 1)
    extended = jnp.concatenate([halo, xbc]).astype(F32)
    xc = conv_shift[None, :]
    for j in range(taps_count):
        xc = xc + conv_kernel[j][None, :] * extended[back - j : back - j + length] * taps[j]
    u = jax.nn.silu(xc)
    x_in, b_in, c_in = u[:, :INNER], u[:, INNER : INNER + STATE], u[:, INNER + STATE :]

    delta_shift = delta_bias.astype(F32)
    rate = jnp.exp(decay_log.astype(F32))
    dt = jax.nn.softplus(delta_raw + delta_shift[None, :])
    log_decay = -dt * rate[None, :]
    places = jnp.arange(length, dtype=jnp.int32)
    lower = (places[:, None] >= places[None, :]).astype(F32)
    cumulative = jnp.dot(lower, log_decay, precision=lax.Precision.HIGHEST)
    final = cumulative[-1]
    carry_gate = jnp.where(seg_own[-1] == seg_before, jnp.exp(final), 0.0)
    rem = jnp.where(seg_col == seg_own[-1], jnp.exp(final[None, :] - cumulative), 0.0)
    ent = jnp.where(seg_col == seg_before, jnp.exp(cumulative), 0.0)
    vec = jnp.stack([dt, cumulative * LOG2E, rem, ent], axis=1)
    vec = vec.reshape(length, 4, GROUPS, GHEADS).transpose(2, 0, 1, 3).reshape(GROUPS, length, 4 * GHEADS)
    row = (cumulative * LOG2E).T
    gate_lanes = jnp.repeat(carry_gate, MHDIM)
    skip_lanes = jnp.repeat(skip_gain.astype(F32), MHDIM)[None, :]

    y_local, state_part = ssd_forward(x_in, b_in, c_in, vec, row, seg_col, seg_row)
    state_in = state_from_behind(gate_lanes, state_part)

    attended, lse = attend(rank_arg, q, keys, values, seg_col, seg_full.reshape(total // length, length))
    attended_low = attended.astype(BF16)

    y, mixed_low = ssd_finish(y_local, x_in, z, c_in, state_in, vec, skip_lanes)
    residual = inputs + dot_nn(mixed_low, w_mo) + dot_nn(attended_low, w_ao)

    r2 = lax.rsqrt(jnp.mean(residual * residual, axis=-1, keepdims=True) + EPSILON)
    n2 = (residual * r2 * gain_two[None, :]).astype(BF16)
    gu = dot_nn(n2, gate_up)
    half = gu.shape[1] // 2
    gate, up = gu[:, :half], gu[:, half:]
    gate_act, gate_slope = silu_parts(gate)
    hidden = (gate_act * up).astype(BF16)
    block_out = (residual + dot_nn(hidden, down)).astype(BF16)

    upstream_low = cotangent[0]
    upstream = upstream_low.astype(F32)
    grad_down = halve(dot_tn(hidden, upstream_low).astype(BF16), order_x)
    dhidden = dot_nt(upstream_low, down)
    dgate = (dhidden * up * gate_slope).astype(BF16)
    dup = (dhidden * gate_act).astype(BF16)
    grad_gate = halve(dot_tn(n2, dgate).astype(BF16), order_y)
    grad_up = halve(dot_tn(n2, dup).astype(BF16), order_z)
    dn2 = dot_nt(dgate, gate_up[:, :half]) + dot_nt(dup, gate_up[:, half:])
    scaled = gain_two[None, :] * dn2
    grad_gain_two = jnp.sum(dn2 * residual * r2, axis=0)
    dhs = upstream + r2 * scaled - residual * (r2 * r2 * r2) * jnp.mean(scaled * residual, axis=-1, keepdims=True)
    dhs_low = dhs.astype(BF16)
    grad_mo = halve(dot_tn(mixed_low, dhs_low).astype(BF16), order_x)
    grad_ao = halve(dot_tn(attended_low, dhs_low).astype(BF16), order_y)
    dym = dot_nt(dhs_low, w_mo)
    do = dot_nt(dhs_low, w_ao).astype(BF16)

    dy, dz, dstate_part, skip_cols = ssd_gate(dym, y, x_in, z, c_in, vec)
    dstate = state_from_ahead(gate_lanes, dstate_part)
    grad_z = halve(dot_tn(n1, dz).astype(BF16), order_y)

    heads = (jnp.arange(QWIDTH)[None, :] // AHDIM == jnp.arange(AHEADS)[:, None]).astype(F32)
    delta = lax.dot_general(
        heads, do.astype(F32) * attended, (((1,), (1,)), ((), ())), precision=lax.Precision.HIGHEST
    )
    dq, dkv = attend_backward(
        rank_arg, q, keys, values, do, lse[:, :AHEADS].T, delta, seg_row, seg_full[:, None]
    )
    own_dkv, more_dkv = scatter_keyval_grads(dkv, length)
    dqkv = unrope(dq, own_dkv, more_dkv, cosine, sine)

    dx, db, dc, cols, rows_sum = ssd_backward(
        x_in, dy, b_in, c_in, state_in, dstate, vec, row, seg_row.T, seg_row, skip_lanes
    )
    direct, leaving, entering, gone = (cols[i, :, :MHEADS] for i in range(4))
    passed = jnp.sum((dstate * state_in).reshape(STATE, MHEADS, MHDIM), axis=(0, 2)) * carry_gate
    change = rows_sum.T - gone + entering - leaving
    upper = (places[:, None] <= places[None, :]).astype(F32)
    da = jnp.dot(upper, change, precision=lax.Precision.HIGHEST)
    da = da + (jnp.sum(leaving, axis=0) + passed)[None, :]
    ddt = direct - da * rate[None, :]
    ddelta = ddt * jax.nn.sigmoid(delta_raw + delta_shift[None, :])
    grad_decay = jnp.sum(da * log_decay, axis=0)
    grad_shift = jnp.sum(ddelta, axis=0)
    grad_skip = jnp.sum(skip_cols.reshape(MHEADS, MHDIM), axis=1)

    _, slope = silu_parts(xc)
    dxc = jnp.concatenate([dx, db, dc], axis=1) * slope
    grad_bias = jnp.sum(dxc, axis=0)
    kernel_rows = []
    spilled = jnp.zeros((length + back, dxc.shape[1]), F32)
    for j in range(taps_count):
        masked = dxc * taps[j]
        kernel_rows.append(jnp.sum(masked * extended[back - j : back - j + length], axis=0))
        spilled = spilled + jnp.pad(masked * conv_kernel[j][None, :], ((back - j, j), (0, 0)))
    incoming = neighbour(spilled[:back], -1)
    dxbc = spilled[back:]
    dxbc = jnp.concatenate([dxbc[: length - back], dxbc[length - back :] + incoming]).astype(BF16)

    kernel_grad = jnp.stack(kernel_rows).reshape(taps_count, count, channels).transpose(1, 0, 2)
    kernel_grad = kernel_grad.reshape(count, taps_count * channels)
    shift_grad = grad_bias.reshape(count, channels)
    head_grads = total_everywhere(jnp.concatenate([grad_shift, grad_decay, grad_skip]))

    def fit_all(value, columns):
        spare = rows * columns - value.shape[1]
        return jnp.pad(value, ((0, 0), (0, spare))).reshape(width, columns)

    ddelta_wide = jnp.pad(ddelta.astype(BF16), ((0, 0), (0, small_width - MHEADS)))
    dq_small = jnp.concatenate([dqkv, ddelta_wide], axis=1)
    dn1 = dot_nt(dq_small, w_q) + dot_nt(dz, w_z) + dot_nt(dxbc, w_x)
    scaled = gain_one[None, :] * dn1
    grad_gain_one = jnp.sum(dn1 * inputs * r1, axis=0)
    grad_tokens = dhs + r1 * scaled - inputs * (r1 * r1 * r1) * jnp.mean(scaled * inputs, axis=-1, keepdims=True)

    grad_qkv = halve(dot_tn(n1, dqkv).astype(BF16), order_z)
    parts = [
        dot_tn(n1, ddelta.astype(BF16)),
        grad_gain_one[:, None],
        grad_gain_two[:, None],
        fit_all(kernel_grad, conv_cols),
        fit_all(shift_grad, bias_cols),
    ]
    used = sum(p.shape[1] for p in parts)
    parts.append(jnp.zeros((width, small_width - used), F32))
    grad_small = halve(jnp.concatenate(parts, axis=1).astype(BF16), order_x)
    cut = 640
    grad_x = jnp.concatenate(
        [
            halve(dot_tn(n1, dxbc[:, :cut]).astype(BF16), order_x),
            halve(dot_tn(n1, dxbc[:, cut : 2 * cut]).astype(BF16), order_y),
            halve(dot_tn(n1, dxbc[:, 2 * cut :]).astype(BF16), order_z),
        ],
        axis=1,
    )

    at = MHEADS + 2
    kernel_own = grad_small[:, at : at + conv_cols].reshape(-1)[: taps_count * channels].reshape(taps_count, channels)
    at += conv_cols
    shift_own = grad_small[:, at : at + bias_cols].reshape(-1)[:channels]
    return (
        block_out[None],
        grad_tokens[None],
        grad_small[:, MHEADS],
        jnp.concatenate([grad_z, grad_x], axis=1),
        grad_small[:, :MHEADS],
        kernel_own,
        shift_own,
        head_grads[:MHEADS],
        head_grads[MHEADS : 2 * MHEADS],
        head_grads[2 * MHEADS :],
        grad_mo,
        grad_qkv,
        grad_ao,
        grad_small[:, MHEADS + 1],
        jnp.concatenate([grad_gate, grad_up], axis=1),
        grad_down,
    )


def solution(mesh):
    both = ("dp", "seq")
    in_specs = (
        P("dp", "seq", None),
        P("dp", None),
        P(both),
        P(both, None),
        P(both, None),
        P(None, both),
        P(both),
        P(),
        P(),
        P(),
        P(both, None),
        P(both, None),
        P(both, None),
        P(both),
        P(both, None),
        P(both, None),
        P("dp", "seq", None),
    )
    out_specs = (
        P("dp", "seq", None),
        P("dp", "seq", None),
        P(both),
        P(both, None),
        P(both, None),
        P(None, both),
        P(both),
        P(),
        P(),
        P(),
        P(both, None),
        P(both, None),
        P(both, None),
        P(both),
        P(both, None),
        P(both, None),
    )
    return jax.shard_map(
        on_device, mesh=mesh, in_specs=in_specs, out_specs=out_specs, check_vma=False
    )
```

```python
import math
from functools import partial

import jax
import jax.numpy as jnp
from jax import lax
from jax.experimental import pallas as pl
from jax.experimental.pallas import tpu as pltpu
from jax.sharding import PartitionSpec as P

MHEADS = 24
MHDIM = 64
STATE = 128
AHEADS = 8
KVHEADS = 2
AHDIM = 64

INNER = MHEADS * MHDIM
CONVD = INNER + 2 * STATE
QWIDTH = AHEADS * AHDIM
KWIDTH = KVHEADS * AHDIM
GROUPS = 3
GHEADS = MHEADS // GROUPS
GLANES = GHEADS * MHDIM
STRIP = 128

EPSILON = 1e-05
ROPE_BASE = 100000000000.0
NEGATIVE = -1e30
LOG2E = math.log2(math.e)

F32 = jnp.float32
BF16 = jnp.bfloat16


def dot_nn(a, b):
    return lax.dot_general(a, b, (((1,), (0,)), ((), ())), preferred_element_type=F32)


def dot_nt(a, b):
    return lax.dot_general(a, b, (((1,), (1,)), ((), ())), preferred_element_type=F32)


def dot_tn(a, b):
    return lax.dot_general(a, b, (((0,), (0,)), ((), ())), preferred_element_type=F32)


def mesh_bits():
    bits = []
    for axis in ("dp", "seq"):
        size = lax.axis_size(axis)
        level = size // 2
        while level:
            bits.append((axis, level))
            level //= 2
    return bits


def bit_orders():
    bits = mesh_bits()
    seq = [b for b in bits if b[0] == "seq"][::-1]
    dp = [b for b in bits if b[0] == "dp"][::-1]
    pair, second, rest = dp[:1], dp[1:2], dp[2:]
    return pair + seq + second + rest, pair + second + seq + rest


def swap(value, bit):
    axis, level = bit
    size = lax.axis_size(axis)
    return lax.ppermute(value, axis, [(i, i ^ level) for i in range(size)])


def bit_here(bit):
    axis, level = bit
    return (lax.axis_index(axis) // level) % 2


def tie(values, arrays):
    return lax.optimization_barrier((values, arrays))


class Halving:
    def __init__(self, full, order):
        self.left = mesh_bits()
        rows = full.shape[0] >> len(self.left)
        self.value = full.reshape((2,) * len(self.left) + (rows, full.shape[1]))
        self.todo = list(order)
        self.bit = self.out = self.got = None

    def prepare(self):
        if self.got is not None:
            place = self.left.index(self.bit)
            kept = lax.dynamic_index_in_dim(self.value, bit_here(self.bit), place, keepdims=False)
            self.left.remove(self.bit)
            value = kept.astype(F32) + self.got.astype(F32)
            self.value = value.astype(BF16) if self.left else value
            self.got = self.out = None
        if self.todo:
            self.bit = self.todo.pop(0)
            place = self.left.index(self.bit)
            self.out = lax.dynamic_index_in_dim(self.value, 1 - bit_here(self.bit), place, keepdims=False)

    def arrays(self):
        return (self.value,) if self.out is None else (self.value, self.out)

    def launch(self, arrays):
        self.value = arrays[0]
        if self.out is not None:
            self.out = arrays[1]
            self.got = swap(self.out, self.bit)


class Doubling:
    def __init__(self, shard, order):
        self.rows, self.columns = shard.shape
        self.value = shard
        self.todo = list(reversed(order))
        self.held = []
        self.bit = self.got = None

    def prepare(self):
        if self.got is not None:
            here = bit_here(self.bit)
            self.held = [b for b in mesh_bits() if b in self.held or b == self.bit]
            place = self.held.index(self.bit)
            own = (jnp.arange(2) == here).reshape((2,) + (1,) * (self.value.ndim - place))
            self.value = jnp.where(own, jnp.expand_dims(self.value, place), jnp.expand_dims(self.got, place))
            self.got = None
        self.bit = self.todo.pop(0) if self.todo else None

    def arrays(self):
        return (self.value,)

    def launch(self, arrays):
        (self.value,) = arrays
        if self.bit is not None:
            self.got = swap(self.value, self.bit)

    def whole(self):
        return self.value.reshape((self.rows << len(self.held), self.columns))


class Summing:
    def __init__(self, value):
        self.value = value
        self.todo = mesh_bits()
        self.bit = self.got = None

    def prepare(self):
        if self.got is not None:
            self.value = self.value + self.got
            self.got = None
        self.bit = self.todo.pop(0) if self.todo else None

    def arrays(self):
        return (self.value,)

    def launch(self, arrays):
        (self.value,) = arrays
        if self.bit is not None:
            self.got = swap(self.value, self.bit)


def step(values, *chains):
    for chain in chains:
        chain.prepare()
    values, arrays = tie(values, [chain.arrays() for chain in chains])
    for chain, own in zip(chains, arrays):
        chain.launch(own)
    return values


def finish(*chains):
    while any(chain.todo or chain.got is not None for chain in chains):
        step((), *chains)


def compose_maps(earlier, later):
    return (later[0] * earlier[0], later[0][None, :] * earlier[1] + later[1])


def state_from_behind(gate, part):
    count = lax.axis_size("seq")
    low = part.astype(BF16)
    if count == 2:
        return lax.ppermute(low, "seq", [(0, 1)]).astype(F32)
    gates = lax.all_gather(gate.astype(BF16), "seq")
    parts = lax.all_gather(low, "seq")
    start = (jnp.ones_like(gate), jnp.zeros_like(part))

    def one(step, state):
        return compose_maps(
            state,
            (
                lax.dynamic_index_in_dim(gates, step, 0, False).astype(F32),
                lax.dynamic_index_in_dim(parts, step, 0, False).astype(F32),
            ),
        )

    return lax.fori_loop(0, lax.axis_index("seq"), one, start)[1]


def state_from_ahead(gate, part):
    count = lax.axis_size("seq")
    low = part.astype(BF16)
    if count == 2:
        return lax.ppermute(low, "seq", [(1, 0)]).astype(F32)
    gates = lax.all_gather(gate.astype(BF16), "seq")
    parts = lax.all_gather(low, "seq")
    start = (jnp.ones_like(gate), jnp.zeros_like(part))
    place = lax.axis_index("seq")

    def one(step, state):
        at = count - 1 - step
        return compose_maps(
            state,
            (
                lax.dynamic_index_in_dim(gates, at, 0, False).astype(F32),
                lax.dynamic_index_in_dim(parts, at, 0, False).astype(F32),
            ),
        )

    return lax.fori_loop(0, count - 1 - place, one, start)[1]


def neighbour(value, steps):
    count = lax.axis_size("seq")
    first, last = (max(0, -steps), min(count, count - steps))
    return lax.ppermute(value, "seq", [(s, s + steps) for s in range(first, last)])


SHORT = pl.CostEstimate(flops=0, bytes_accessed=0, transcendentals=0)
PARAMS = pltpu.CompilerParams(vmem_limit_bytes=48 * 1024 * 1024)


def group_columns(vec_ref, which):
    shift = lax.rem(128 - pl.program_id(0) * GHEADS, 128)
    return pltpu.roll(vec_ref[which], shift, 1)


def lane_is_low(rows):
    return lax.broadcasted_iota(jnp.int32, (rows, 128), 1) < MHDIM


def spread(low, vec, head):
    return jnp.where(low, vec[:, head : head + 1], vec[:, head + 1 : head + 2])


def ssd_forward_kernel(x_ref, b_ref, c_ref, vec_ref, row_ref, segc_ref, segr_ref, y_ref, st_ref, cb_ref, cum_ref):
    length = x_ref.shape[0]

    @pl.when(pl.program_id(0) == 0)
    def _():
        t = lax.broadcasted_iota(jnp.int32, (length, length), 0)
        s = lax.broadcasted_iota(jnp.int32, (length, length), 1)
        seen = (t >= s) & (segc_ref[...] == segr_ref[...])
        cb = dot_nt(c_ref[...].astype(BF16), b_ref[...].astype(BF16))
        cb_ref[...] = jnp.where(seen, cb, 0.0)

    b_low = b_ref[...].astype(BF16)
    wide = lane_is_low(length)
    narrow = lane_is_low(STRIP)
    dt = group_columns(vec_ref, 0)
    rem = group_columns(vec_ref, 2)
    cum_ref[...] = group_columns(vec_ref, 1)
    for pair in range(GHEADS // 2):
        lanes = slice(pair * 128, (pair + 1) * 128)
        xd = x_ref[:, lanes] * spread(wide, dt, 2 * pair)
        xd_low = xd.astype(BF16)
        st_ref[:, lanes] = dot_tn(b_low, (xd * spread(wide, rem, 2 * pair)).astype(BF16))
        for strip in range(length // STRIP):
            first, width = strip * STRIP, (strip + 1) * STRIP
            halves = []
            for head in (2 * pair, 2 * pair + 1):
                gap = cum_ref[first : first + STRIP, head : head + 1] - row_ref[head : head + 1, :width]
                decay = jnp.exp2(jnp.minimum(gap, 0.0))
                m = (decay * cb_ref[first : first + STRIP, :width]).astype(BF16)
                halves.append(dot_nn(m, xd_low[:width]))
            y_ref[first : first + STRIP, lanes] = jnp.where(narrow, halves[0], halves[1])


def group_specs(length):
    x_spec = pl.BlockSpec((length, GLANES), lambda g: (0, g))
    s_spec = pl.BlockSpec((STATE, GLANES), lambda g: (0, g))
    n_spec = pl.BlockSpec((length, STATE), lambda g: (0, 0))
    b_spec = pl.BlockSpec((length, STATE), lambda g: (0, INNER // STATE))
    c_spec = pl.BlockSpec((length, STATE), lambda g: (0, INNER // STATE + 1))
    v_spec = pl.BlockSpec((4, length, 128), lambda g: (0, 0, 0))
    r_spec = pl.BlockSpec((GHEADS, length), lambda g: (g, 0))
    return x_spec, s_spec, n_spec, b_spec, c_spec, v_spec, r_spec


def ssd_forward(x, b, c, vec, row, seg_col, seg_row):
    length = x.shape[0]
    x_spec, s_spec, n_spec, b_spec, c_spec, v_spec, r_spec = group_specs(length)
    return pl.pallas_call(
        ssd_forward_kernel,
        grid=(GROUPS,),
        in_specs=[
            x_spec, b_spec, c_spec, v_spec, r_spec,
            pl.BlockSpec((length, 1), lambda g: (0, 0)),
            pl.BlockSpec((1, length), lambda g: (0, 0)),
        ],
        out_specs=[x_spec, s_spec],
        out_shape=[
            jax.ShapeDtypeStruct((length, INNER), F32),
            jax.ShapeDtypeStruct((STATE, INNER), F32),
        ],
        scratch_shapes=[pltpu.VMEM((length, length), F32), pltpu.VMEM((length, 128), F32)],
        compiler_params=PARAMS,
        cost_estimate=SHORT,
        name="ssd_forward",
    )(x, b, c, vec, row, seg_col, seg_row)


def silu_parts(v):
    sig = 1.0 / (1.0 + jnp.exp(-v))
    return v * sig, sig * (1.0 + v * (1.0 - sig))


def ssd_finish_kernel(y0_ref, x_ref, z_ref, c_ref, st_ref, vec_ref, skip_ref, y_ref, ym_ref):
    length = x_ref.shape[0]
    wide = lane_is_low(length)
    ent = group_columns(vec_ref, 3)
    c_low = c_ref[...].astype(BF16)
    for pair in range(GHEADS // 2):
        lanes = slice(pair * 128, (pair + 1) * 128)
        cs = dot_nn(c_low, st_ref[:, lanes].astype(BF16))
        y = y0_ref[:, lanes] + spread(wide, ent, 2 * pair) * cs + skip_ref[:, lanes] * x_ref[:, lanes]
        gate, _ = silu_parts(z_ref[:, lanes].astype(F32))
        y_ref[:, lanes] = y
        ym_ref[:, lanes] = (y * gate).astype(BF16)


def ssd_finish(y0, x, z, c, state, vec, skip):
    length = x.shape[0]
    x_spec, s_spec, n_spec, b_spec, c_spec, v_spec, _ = group_specs(length)
    return pl.pallas_call(
        ssd_finish_kernel,
        grid=(GROUPS,),
        in_specs=[x_spec, x_spec, x_spec, c_spec, s_spec, v_spec, pl.BlockSpec((1, GLANES), lambda g: (0, g))],
        out_specs=[x_spec, x_spec],
        out_shape=[
            jax.ShapeDtypeStruct((length, INNER), F32),
            jax.ShapeDtypeStruct((length, INNER), BF16),
        ],
        compiler_params=PARAMS,
        cost_estimate=SHORT,
        name="ssd_finish",
    )(y0, x, z, c, state, vec, skip)


def ssd_gate_kernel(dym_ref, y_ref, x_ref, z_ref, c_ref, vec_ref, dy_ref, dz_ref, ds_ref, skip_ref):
    length = x_ref.shape[0]
    wide = lane_is_low(length)
    ent = group_columns(vec_ref, 3)
    c_low = c_ref[...].astype(BF16)
    for pair in range(GHEADS // 2):
        lanes = slice(pair * 128, (pair + 1) * 128)
        gate, slope = silu_parts(z_ref[:, lanes].astype(F32))
        dym = dym_ref[:, lanes]
        dy = dym * gate
        dy_ref[:, lanes] = dy
        dz_ref[:, lanes] = (dym * y_ref[:, lanes] * slope).astype(BF16)
        ds_ref[:, lanes] = dot_tn(c_low, (dy * spread(wide, ent, 2 * pair)).astype(BF16))
        skip_ref[:, lanes] = jnp.sum(dy * x_ref[:, lanes], axis=0, keepdims=True)


def ssd_gate(dym, y, x, z, c, vec):
    length = x.shape[0]
    x_spec, s_spec, n_spec, b_spec, c_spec, v_spec, _ = group_specs(length)
    one_spec = pl.BlockSpec((1, GLANES), lambda g: (0, g))
    return pl.pallas_call(
        ssd_gate_kernel,
        grid=(GROUPS,),
        in_specs=[x_spec, x_spec, x_spec, x_spec, c_spec, v_spec],
        out_specs=[x_spec, x_spec, s_spec, one_spec],
        out_shape=[
            jax.ShapeDtypeStruct((length, INNER), F32),
            jax.ShapeDtypeStruct((length, INNER), BF16),
            jax.ShapeDtypeStruct((STATE, INNER), F32),
            jax.ShapeDtypeStruct((1, INNER), F32),
        ],
        compiler_params=PARAMS,
        cost_estimate=SHORT,
        name="ssd_gate",
    )(dym, y, x, z, c, vec)


def ssd_backward_kernel(
    x_ref, dy_ref, b_ref, c_ref, st_ref, dst_ref, vec_ref, row_ref, segc_ref, segr_ref, skip_ref,
    dx_ref, db_ref, dc_ref, cols_ref, rows_ref, bc_ref, dbc_ref, xd_ref, sum_ref, cum_ref,
):
    length = x_ref.shape[0]
    group = pl.program_id(0)

    @pl.when(group == 0)
    def _():
        s = lax.broadcasted_iota(jnp.int32, (length, length), 0)
        t = lax.broadcasted_iota(jnp.int32, (length, length), 1)
        seen = (t >= s) & (segc_ref[...] == segr_ref[...])
        bc = dot_nt(b_ref[...].astype(BF16), c_ref[...].astype(BF16))
        bc_ref[...] = jnp.where(seen, bc, 0.0)
        dbc_ref[...] = jnp.zeros_like(dbc_ref)
        db_ref[...] = jnp.zeros_like(db_ref)
        dc_ref[...] = jnp.zeros_like(dc_ref)
        cols_ref[...] = jnp.zeros_like(cols_ref)

    b_low = b_ref[...].astype(BF16)
    c_low = c_ref[...].astype(BF16)
    wide = lane_is_low(length)
    narrow = lane_is_low(STRIP)
    lane = lax.broadcasted_iota(jnp.int32, (STRIP, 128), 1)
    spot = lax.broadcasted_iota(jnp.int32, (128, 128), 0) // MHDIM
    place = lax.broadcasted_iota(jnp.int32, (128, 128), 1)
    dt = group_columns(vec_ref, 0)
    rem = group_columns(vec_ref, 2)
    ent = group_columns(vec_ref, 3)
    cum_ref[...] = group_columns(vec_ref, 1)
    rows_ref[...] = jnp.zeros_like(rows_ref)
    for pair in range(GHEADS // 2):
        lanes = slice(pair * 128, (pair + 1) * 128)
        x = x_ref[:, lanes]
        dy = dy_ref[:, lanes]
        dtx = spread(wide, dt, 2 * pair)
        remx = spread(wide, rem, 2 * pair)
        entx = spread(wide, ent, 2 * pair)
        dy_low = dy.astype(BF16)
        xd_ref[...] = (x * dtx).astype(BF16)
        st_low = st_ref[:, lanes].astype(BF16)
        dst_low = dst_ref[:, lanes].astype(BF16)
        carried = remx * dot_nn(b_low, dst_low)
        entered = entx * dot_nn(c_low, st_low)
        dc_ref[...] += dot_nt((entx * dy).astype(BF16), st_low)
        db_ref[...] += dot_nt((dtx * remx * x).astype(BF16), dst_low)
        for strip in range(length // STRIP):
            first = strip * STRIP
            xd = xd_ref[first : first + STRIP, :]
            dys = dy_low[first:]
            halves = []
            for half in range(2):
                head = 2 * pair + half
                mine = narrow if half == 0 else ~narrow
                gap = row_ref[head : head + 1, first:] - cum_ref[first : first + STRIP, head : head + 1]
                decay = jnp.exp2(jnp.minimum(gap, 0.0))
                bc = bc_ref[first : first + STRIP, first:]
                m = (decay * bc).astype(BF16)
                halves.append(dot_nn(m, dys))
                dg = decay * dot_nt(jnp.where(mine, xd, jnp.zeros_like(xd)), dys)
                dbc_ref[first : first + STRIP, first:] += dg
                e = dg * bc
                rows_ref[head : head + 1, first:] += jnp.sum(e, axis=0, keepdims=True)
                gone = jnp.sum(e, axis=1, keepdims=True)
                at = group * GHEADS + head
                cols_ref[3, first : first + STRIP, :] += jnp.where(lane == at, gone, 0.0)
            dxd = jnp.where(narrow, halves[0], halves[1]) + carried[first : first + STRIP]
            sum_ref[first : first + STRIP, :] = dxd
        dxd = sum_ref[...]
        dx_ref[:, lanes] = dtx * dxd + skip_ref[:, lanes] * dy
        pick = (place == group * GHEADS + 2 * pair + spot).astype(BF16)

        def per_head(value):
            high = value.astype(BF16)
            rest = (value - high.astype(F32)).astype(BF16)
            return dot_nn(high, pick) + dot_nn(rest, pick)

        cols_ref[0] += per_head(dxd * x)
        cols_ref[1] += per_head(dtx * x * carried)
        cols_ref[2] += per_head(dy * entered)
        passed = jnp.sum(st_ref[:, lanes] * dst_ref[:, lanes], axis=0, keepdims=True) * entx[length - 1 :]
        cols_ref[2, length - 8 :, :] += jnp.where(
            lax.broadcasted_iota(jnp.int32, (8, 128), 0) == 7, per_head(jnp.broadcast_to(passed, (8, 128))), 0.0
        )

    @pl.when(group == GROUPS - 1)
    def _():
        s = lax.broadcasted_iota(jnp.int32, (length, length), 0)
        t = lax.broadcasted_iota(jnp.int32, (length, length), 1)
        seen = (t >= s) & (segc_ref[...] == segr_ref[...])
        dbc = jnp.where(seen, dbc_ref[...], 0.0).astype(BF16)
        db_ref[...] += dot_nn(dbc, c_low)
        dc_ref[...] += dot_tn(dbc, b_low)


def ssd_backward(x, dy, b, c, state, dstate, vec, row, seg_col, seg_row, skip):
    length = x.shape[0]
    x_spec, s_spec, n_spec, b_spec, c_spec, v_spec, r_spec = group_specs(length)
    return pl.pallas_call(
        ssd_backward_kernel,
        grid=(GROUPS,),
        in_specs=[
            x_spec, x_spec, b_spec, c_spec, s_spec, s_spec, v_spec, r_spec,
            pl.BlockSpec((length, 1), lambda g: (0, 0)),
            pl.BlockSpec((1, length), lambda g: (0, 0)),
            pl.BlockSpec((1, GLANES), lambda g: (0, g)),
        ],
        out_specs=[x_spec, n_spec, n_spec, pl.BlockSpec((4, length, 128), lambda g: (0, 0, 0)), r_spec],
        out_shape=[
            jax.ShapeDtypeStruct((length, INNER), F32),
            jax.ShapeDtypeStruct((length, STATE), F32),
            jax.ShapeDtypeStruct((length, STATE), F32),
            jax.ShapeDtypeStruct((4, length, 128), F32),
            jax.ShapeDtypeStruct((MHEADS, length), F32),
        ],
        scratch_shapes=[
            pltpu.VMEM((length, length), F32),
            pltpu.VMEM((length, length), F32),
            pltpu.VMEM((length, 128), BF16),
            pltpu.VMEM((length, 128), F32),
            pltpu.VMEM((length, 128), F32),
        ],
        compiler_params=PARAMS,
        cost_estimate=SHORT,
        name="ssd_backward",
    )(x, dy, b, c, state, dstate, vec, row, seg_col, seg_row, skip)


def conv_of(ext_ref, kernel_ref, taps_ref, taps_count):
    length = taps_ref.shape[0]
    total = jnp.zeros((length, ext_ref.shape[1]), F32) + kernel_ref[taps_count : taps_count + 1, :]
    for j in range(taps_count):
        total = total + kernel_ref[j : j + 1, :] * ext_ref[8 - j : 8 - j + length, :] * taps_ref[:, j : j + 1]
    return total


def conv_kernel_body(taps_count, xbc_ref, halo_ref, kernel_ref, taps_ref, u_ref, ext_ref):
    ext_ref[:8, :] = halo_ref[...]
    ext_ref[8:, :] = xbc_ref[...].astype(F32)
    xc = conv_of(ext_ref, kernel_ref, taps_ref, taps_count)
    u_ref[...] = silu_parts(xc)[0]


def conv_forward(xbc, halo, kernel, taps, taps_count):
    length, channels = xbc.shape
    wide = 256
    spec = pl.BlockSpec((length, wide), lambda g: (0, g))
    eight = pl.BlockSpec((8, wide), lambda g: (0, g))
    return pl.pallas_call(
        partial(conv_kernel_body, taps_count),
        grid=(channels // wide,),
        in_specs=[spec, eight, eight, pl.BlockSpec((length, 8), lambda g: (0, 0))],
        out_specs=spec,
        out_shape=jax.ShapeDtypeStruct((length, channels), F32),
        scratch_shapes=[pltpu.VMEM((length + 8, wide), F32)],
        compiler_params=PARAMS,
        cost_estimate=SHORT,
        name="conv_forward",
    )(xbc, halo, kernel, taps)


def conv_backward_body(
    taps_count, dx_ref, db_ref, dc_ref, xbc_ref, halo_ref, kernel_ref, taps_ref,
    out_ref, last_ref, spill_ref, grad_ref, ext_ref, du_ref, put_ref, mask_ref,
):
    length = taps_ref.shape[0]
    block = pl.program_id(0)
    heads_blocks = INNER // 128

    @pl.when(block == 0)
    def _():
        for j in range(taps_count):
            mask_ref[j] = jnp.broadcast_to(taps_ref[:, j : j + 1], (length, 128))

    @pl.when(block < heads_blocks)
    def _():
        du_ref[...] = dx_ref[...]

    @pl.when(block == heads_blocks)
    def _():
        du_ref[...] = db_ref[...]

    @pl.when(block == heads_blocks + 1)
    def _():
        du_ref[...] = dc_ref[...]

    ext_ref[:8, :] = halo_ref[...]
    ext_ref[8:, :] = xbc_ref[...].astype(F32)
    xc = jnp.zeros((length, 128), F32) + kernel_ref[taps_count : taps_count + 1, :]
    for j in range(taps_count):
        xc = xc + kernel_ref[j : j + 1, :] * ext_ref[8 - j : 8 - j + length, :] * mask_ref[j]
    dxc = du_ref[...] * silu_parts(xc)[1]
    put_ref[:8, :] = jnp.zeros((8, 128), F32)
    put_ref[8 + length :, :] = jnp.zeros((8, 128), F32)
    total = jnp.zeros((length + 8, 128), F32)
    sums = []
    for j in range(taps_count):
        masked = dxc * mask_ref[j]
        sums.append(jnp.sum(masked * ext_ref[8 - j : 8 - j + length, :], axis=0, keepdims=True))
        put_ref[8 : 8 + length, :] = masked * kernel_ref[j : j + 1, :]
        total = total + put_ref[j : j + length + 8, :]
    sums.append(jnp.sum(dxc, axis=0, keepdims=True))
    sums.append(jnp.zeros((7 - taps_count, 128), F32))
    spill_ref[...] = total[:8]
    out_ref[...] = total[8:].astype(BF16)
    last_ref[...] = total[length:]
    grad_ref[...] = jnp.concatenate(sums, axis=0)


def conv_backward(dx, db, dc, xbc, halo, kernel, taps, taps_count):
    length, channels = xbc.shape
    last = INNER // 128 - 1
    spec = pl.BlockSpec((length, 128), lambda g: (0, g))
    whole = pl.BlockSpec((length, 128), lambda g: (0, 0))
    eight = pl.BlockSpec((8, 128), lambda g: (0, g))
    return pl.pallas_call(
        partial(conv_backward_body, taps_count),
        grid=(channels // 128,),
        in_specs=[
            pl.BlockSpec((length, 128), lambda g: (0, jnp.minimum(g, last))), whole, whole,
            spec, eight, eight, pl.BlockSpec((length, 8), lambda g: (0, 0)),
        ],
        out_specs=[spec, eight, eight, eight],
        out_shape=[
            jax.ShapeDtypeStruct((length, channels), BF16),
            jax.ShapeDtypeStruct((8, channels), F32),
            jax.ShapeDtypeStruct((8, channels), F32),
            jax.ShapeDtypeStruct((8, channels), F32),
        ],
        scratch_shapes=[
            pltpu.VMEM((length + 8, 128), F32),
            pltpu.VMEM((length, 128), F32),
            pltpu.VMEM((length + 16, 128), F32),
            pltpu.VMEM((taps_count, length, 128), F32),
        ],
        compiler_params=PARAMS,
        cost_estimate=SHORT,
        name="conv_backward",
    )(dx, db, dc, xbc, halo, kernel, taps)


def softplus(v):
    return jnp.maximum(v, 0.0) + jnp.log1p(jnp.exp(-jnp.abs(v)))


def exact_dot(a, b):
    return lax.dot_general(
        a, b, (((1,), (0,)), ((), ())), precision=lax.Precision.HIGHEST, preferred_element_type=F32
    )


def head_values(raw_ref, heads_ref):
    real = lax.broadcasted_iota(jnp.int32, raw_ref.shape, 1) < MHEADS
    shifted = jnp.where(real, raw_ref[...] + heads_ref[0:1, :], 0.0)
    dt = jnp.where(real, softplus(shifted), 0.0)
    rate = jnp.exp(heads_ref[1:2, :])
    return shifted, dt, rate, -dt * rate


def heads_kernel(before_ref, raw_ref, heads_ref, seg_ref, vec_ref, row_ref):
    length = raw_ref.shape[0]
    _, dt, _, log_decay = head_values(raw_ref, heads_ref)
    t = lax.broadcasted_iota(jnp.int32, (length, length), 0)
    s = lax.broadcasted_iota(jnp.int32, (length, length), 1)
    cumulative = exact_dot(jnp.where(t >= s, 1.0, 0.0), log_decay)
    final = cumulative[length - 1 :]
    seg = seg_ref[...]
    vec_ref[0] = dt
    vec_ref[1] = cumulative * LOG2E
    vec_ref[2] = jnp.where(seg == seg[length - 1 :], jnp.exp(final - cumulative), 0.0)
    vec_ref[3] = jnp.where(seg == before_ref[0], jnp.exp(cumulative), 0.0)
    row_ref[...] = (cumulative * LOG2E).T


def heads_forward(before, raw, heads, seg_col):
    length = raw.shape[0]
    vmem = pl.BlockSpec(memory_space=pltpu.VMEM)
    return pl.pallas_call(
        heads_kernel,
        in_specs=[pl.BlockSpec(memory_space=pltpu.SMEM)] + [vmem] * 3,
        out_specs=[vmem, vmem],
        out_shape=[
            jax.ShapeDtypeStruct((4, length, 128), F32),
            jax.ShapeDtypeStruct((128, length), F32),
        ],
        compiler_params=PARAMS,
        cost_estimate=SHORT,
        name="heads_forward",
    )(before, raw, heads, seg_col)


def heads_backward_kernel(raw_ref, heads_ref, cols_ref, rows_ref, low_ref, sums_ref):
    length = raw_ref.shape[0]
    shifted, _, rate, log_decay = head_values(raw_ref, heads_ref)
    filler = jnp.zeros((128 - MHEADS, length), F32)
    gained = jnp.concatenate([rows_ref[...], filler], axis=0).T
    leaving = cols_ref[1]
    change = gained - cols_ref[3] + cols_ref[2] - leaving
    t = lax.broadcasted_iota(jnp.int32, (length, length), 0)
    s = lax.broadcasted_iota(jnp.int32, (length, length), 1)
    da = exact_dot(jnp.where(t <= s, 1.0, 0.0), change) + jnp.sum(leaving, axis=0, keepdims=True)
    real = lax.broadcasted_iota(jnp.int32, raw_ref.shape, 1) < MHEADS
    ddelta = jnp.where(real, (cols_ref[0] - da * rate) / (1.0 + jnp.exp(-shifted)), 0.0)
    low_ref[...] = ddelta.astype(BF16)
    sums_ref[...] = jnp.concatenate(
        [
            jnp.sum(ddelta, axis=0, keepdims=True),
            jnp.sum(da * log_decay, axis=0, keepdims=True),
            jnp.zeros((6, 128), F32),
        ],
        axis=0,
    )


def heads_backward(raw, heads, cols, rows):
    length = raw.shape[0]
    return pl.pallas_call(
        heads_backward_kernel,
        out_shape=[
            jax.ShapeDtypeStruct((length, 128), BF16),
            jax.ShapeDtypeStruct((8, 128), F32),
        ],
        compiler_params=PARAMS,
        cost_estimate=SHORT,
        name="heads_backward",
    )(raw, heads, cols, rows)


def turn(value, cosine, sine):
    low = (lax.broadcasted_iota(jnp.int32, value.shape, 1) % AHDIM) < AHDIM // 2
    other = jnp.where(low, pltpu.roll(value, 128 - AHDIM // 2, 1), pltpu.roll(value, AHDIM // 2, 1))
    return value * cosine + other * sine


def rope_kernel(qkv_ref, cos_ref, sin_ref, q_ref, kv_ref):
    cosine, sine = cos_ref[...], sin_ref[...]
    scale = AHDIM ** (-0.5)
    for at in range(QWIDTH // 128):
        lanes = slice(at * 128, (at + 1) * 128)
        q_ref[:, lanes] = (turn(qkv_ref[:, lanes], cosine, sine).astype(BF16).astype(F32) * scale).astype(BF16)
    kv_ref[:, :KWIDTH] = turn(qkv_ref[:, QWIDTH : QWIDTH + KWIDTH], cosine, sine).astype(BF16)
    kv_ref[:, KWIDTH:] = qkv_ref[:, QWIDTH + KWIDTH :].astype(BF16)


def rope(qkv, cosine, sine):
    length = qkv.shape[0]
    return pl.pallas_call(
        rope_kernel,
        out_shape=[
            jax.ShapeDtypeStruct((length, QWIDTH), BF16),
            jax.ShapeDtypeStruct((length, 2 * KWIDTH), BF16),
        ],
        compiler_params=PARAMS,
        cost_estimate=SHORT,
        name="rope",
    )(qkv, cosine, sine)


def unrope_kernel(dq_ref, dkv_ref, more_ref, cos_ref, sin_ref, out_ref):
    cosine, sine = cos_ref[...], -sin_ref[...]
    scale = AHDIM ** (-0.5)
    for at in range(QWIDTH // 128):
        lanes = slice(at * 128, (at + 1) * 128)
        out_ref[:, lanes] = (turn(dq_ref[:, lanes], cosine, sine) * scale).astype(BF16)
    dkv = dkv_ref[...] + more_ref[...].astype(F32)
    out_ref[:, QWIDTH : QWIDTH + KWIDTH] = turn(dkv[:, :KWIDTH], cosine, sine).astype(BF16)
    out_ref[:, QWIDTH + KWIDTH :] = dkv[:, KWIDTH:].astype(BF16)


def unrope(dq, dkv, more, cosine, sine):
    length = dq.shape[0]
    return pl.pallas_call(
        unrope_kernel,
        out_shape=jax.ShapeDtypeStruct((length, QWIDTH + 2 * KWIDTH), BF16),
        compiler_params=PARAMS,
        cost_estimate=SHORT,
        name="unrope",
    )(dq, dkv, more, cosine, sine)


def repeat_heads(kv_ref, k_ref, v_ref):
    low = lane_is_low(kv_ref.shape[0])
    for start, out in ((0, k_ref), (KWIDTH, v_ref)):
        own = kv_ref[:, start : start + KWIDTH].astype(F32)
        moved = pltpu.roll(own, AHDIM, 1)
        out[0] = jnp.where(low, own, moved).astype(BF16)
        out[1] = jnp.where(low, moved, own).astype(BF16)


def attend_kernel(rank_ref, q_ref, kv_ref, segq_ref, segk_ref, o_ref, lse_ref, top_ref, sum_ref, acc_ref, mask_ref, k_ref, v_ref):
    length = q_ref.shape[0]
    repeat_heads(kv_ref, k_ref, v_ref)
    rank = rank_ref[0]
    top_ref[...] = jnp.full_like(top_ref, NEGATIVE)
    sum_ref[...] = jnp.zeros_like(sum_ref)
    acc_ref[...] = jnp.zeros_like(acc_ref)
    narrow = lane_is_low(STRIP)

    def block(step, carry):
        at = rank - step
        t = lax.broadcasted_iota(jnp.int32, (length, length), 0) + rank * length
        s = lax.broadcasted_iota(jnp.int32, (length, length), 1) + at * length
        seen = (s <= t) & (segq_ref[...] == segk_ref[pl.ds(at, 1), :])
        mask_ref[...] = jnp.where(seen, 0.0, NEGATIVE)
        start = pl.multiple_of(at * length, length)
        for head in range(AHEADS):
            kv_head = head // (AHEADS // KVHEADS)
            mine = narrow if head % 2 == 0 else ~narrow
            lanes = slice(head // 2 * 128, (head // 2 + 1) * 128)
            keys = k_ref[kv_head, pl.ds(start, length), :]
            values = v_ref[kv_head, pl.ds(start, length), :]
            for strip in range(length // STRIP):
                rows = slice(strip * STRIP, (strip + 1) * STRIP)
                q = q_ref[rows, lanes]
                scores = dot_nt(jnp.where(mine, q, jnp.zeros_like(q)), keys) + mask_ref[rows, :]
                old = top_ref[head, rows, :]
                new = jnp.maximum(old, jnp.max(scores, axis=1, keepdims=True))
                fade = jnp.exp(old - new)
                probs = jnp.exp(scores - new[:, :1])
                sum_ref[head, rows, :] = sum_ref[head, rows, :] * fade + jnp.sum(probs, axis=1, keepdims=True)
                top_ref[head, rows, :] = new
                acc = acc_ref[rows, lanes]
                acc_ref[rows, lanes] = jnp.where(mine, acc * fade + dot_nn(probs.astype(BF16), values), acc)
        return carry

    lax.fori_loop(0, rank + 1, block, 0)
    lane = lax.broadcasted_iota(jnp.int32, (length, 128), 1)
    stats = jnp.zeros((length, 128), F32)
    low = lane_is_low(length)
    for pair in range(AHEADS // 2):
        lanes = slice(pair * 128, (pair + 1) * 128)
        o_ref[:, lanes] = acc_ref[:, lanes] / jnp.where(low, sum_ref[2 * pair], sum_ref[2 * pair + 1])
    for head in range(AHEADS):
        stats = jnp.where(lane == head, top_ref[head] + jnp.log(sum_ref[head]), stats)
    lse_ref[...] = stats


def attend(rank, q, keyvals, seg_col, seg_blocks):
    length, total = q.shape[0], keyvals.shape[0]
    vmem = pl.BlockSpec(memory_space=pltpu.VMEM)
    return pl.pallas_call(
        attend_kernel,
        in_specs=[pl.BlockSpec(memory_space=pltpu.SMEM)] + [vmem] * 4,
        out_specs=[vmem, vmem],
        out_shape=[
            jax.ShapeDtypeStruct((length, QWIDTH), F32),
            jax.ShapeDtypeStruct((length, 128), F32),
        ],
        scratch_shapes=[
            pltpu.VMEM((AHEADS, length, 128), F32),
            pltpu.VMEM((AHEADS, length, 128), F32),
            pltpu.VMEM((length, QWIDTH), F32),
            pltpu.VMEM((length, length), F32),
            pltpu.VMEM((KVHEADS, total, 128), BF16),
            pltpu.VMEM((KVHEADS, total, 128), BF16),
        ],
        compiler_params=PARAMS,
        cost_estimate=SHORT,
        name="attend",
    )(rank, q, keyvals, seg_col, seg_blocks)


def attend_backward_kernel(
    rank_ref, q_ref, kv_ref, do_ref, lse_ref, delta_ref, segq_ref, segk_ref, dq_ref, dkv_ref, k_ref, v_ref
):
    length = q_ref.shape[0]
    repeat_heads(kv_ref, k_ref, v_ref)
    rank = rank_ref[0]
    dq_ref[...] = jnp.zeros_like(dq_ref)
    dkv_ref[...] = jnp.zeros_like(dkv_ref)
    narrow = lane_is_low(STRIP)
    per = AHEADS // KVHEADS

    def strip_of(step, carry):
        start = pl.multiple_of(step * STRIP, STRIP)
        s = lax.broadcasted_iota(jnp.int32, (STRIP, length), 0) + start
        t = lax.broadcasted_iota(jnp.int32, (STRIP, length), 1) + rank * length
        seen = (s <= t) & (segk_ref[pl.ds(start, STRIP), :] == segq_ref[...])
        mask = jnp.where(seen, 0.0, NEGATIVE)
        sums = []
        for kv_head in range(KVHEADS):
            keys = k_ref[kv_head, pl.ds(start, STRIP), :]
            values = v_ref[kv_head, pl.ds(start, STRIP), :]
            dk = jnp.zeros((STRIP, 128), F32)
            dv = jnp.zeros((STRIP, 128), F32)
            for head in range(kv_head * per, (kv_head + 1) * per):
                mine = narrow if head % 2 == 0 else ~narrow
                lanes = slice(head // 2 * 128, (head // 2 + 1) * 128)
                q = q_ref[:, lanes]
                do = do_ref[:, lanes]
                own_keys = jnp.where(mine, keys, jnp.zeros_like(keys))
                own_values = jnp.where(mine, values, jnp.zeros_like(values))
                probs = jnp.exp(dot_nt(own_keys, q) + mask - lse_ref[head : head + 1, :])
                dp = dot_nt(own_values, do)
                ds = (probs * (dp - delta_ref[head : head + 1, :])).astype(BF16)
                dv += jnp.where(mine, dot_nn(probs.astype(BF16), do), 0.0)
                dk += jnp.where(mine, dot_nn(ds, q), 0.0)
                dq_ref[:, lanes] += dot_tn(ds, own_keys)
            sums.append((dk + pltpu.roll(dk, AHDIM, 1), dv + pltpu.roll(dv, AHDIM, 1)))
        dkv_ref[pl.ds(start, STRIP), :KWIDTH] = jnp.where(narrow, sums[0][0], sums[1][0])
        dkv_ref[pl.ds(start, STRIP), KWIDTH:] = jnp.where(narrow, sums[0][1], sums[1][1])
        return carry

    lax.fori_loop(0, (rank + 1) * (length // STRIP), strip_of, 0)


def attend_backward(rank, q, keyvals, do, lse, delta, seg_row, seg_keys):
    length, total = q.shape[0], keyvals.shape[0]
    vmem = pl.BlockSpec(memory_space=pltpu.VMEM)
    return pl.pallas_call(
        attend_backward_kernel,
        in_specs=[pl.BlockSpec(memory_space=pltpu.SMEM)] + [vmem] * 7,
        out_specs=[vmem, vmem],
        out_shape=[
            jax.ShapeDtypeStruct((length, QWIDTH), F32),
            jax.ShapeDtypeStruct((total, 2 * KWIDTH), F32),
        ],
        scratch_shapes=[
            pltpu.VMEM((KVHEADS, total, 128), BF16),
            pltpu.VMEM((KVHEADS, total, 128), BF16),
        ],
        compiler_params=PARAMS,
        cost_estimate=SHORT,
        name="attend_backward",
    )(rank, q, keyvals, do, lse, delta, seg_row, seg_keys)


def gather_keyvals(own):
    count = lax.axis_size("seq")
    if count == 2:
        got = lax.ppermute(own, "seq", [(0, 1)])
        first = lax.axis_index("seq") == 0
        return jnp.concatenate([jnp.where(first, own, got), own])
    return lax.all_gather(own, "seq", axis=0, tiled=True)


def scatter_keyval_grads(grads, length):
    count = lax.axis_size("seq")
    place = lax.axis_index("seq")
    if count == 2:
        own = lax.dynamic_slice_in_dim(grads, place * length, length)
        return own, lax.ppermute(grads[:length].astype(BF16), "seq", [(1, 0)])
    total = lax.psum_scatter(grads.astype(BF16), "seq", scatter_dimension=0, tiled=True)
    return jnp.zeros((length, grads.shape[1]), F32), total


def fit(value, rows):
    flat = value.reshape(-1)
    columns = -(-flat.shape[0] // rows)
    return jnp.pad(flat, (0, rows * columns - flat.shape[0])).reshape(rows, columns)


def on_device(
    tokens,
    segment_ids,
    norm1_gain,
    w_mamba_in,
    w_delta,
    conv_weight,
    conv_bias,
    delta_bias,
    decay_log,
    skip_gain,
    w_mamba_out,
    w_qkv,
    w_attn_out,
    norm2_gain,
    w_gate_up,
    w_down,
    cotangent,
):
    order_x, order_y = bit_orders()
    count = lax.axis_size("dp") * lax.axis_size("seq")
    rows = w_qkv.shape[0]
    width = rows * count
    taps_count, channels = conv_weight.shape
    conv_cols = -(-taps_count * channels // rows)
    bias_cols = -(-channels // rows)
    small = jnp.concatenate(
        [w_delta, norm1_gain[:, None], norm2_gain[:, None], fit(conv_weight, rows), fit(conv_bias, rows)], axis=1
    )
    small_width = 128 * (-(-small.shape[1] // 128))
    small = jnp.pad(small, ((0, 0), (0, small_width - small.shape[1])))

    packed = jnp.concatenate([w_mamba_in, w_qkv, small], axis=1)
    w_in = lax.all_gather(packed, ("dp", "seq"), axis=0, tiled=True)
    second = [Doubling(w_mamba_out, order_x), Doubling(w_attn_out, order_y)]
    third = Doubling(w_down, order_y)
    while len(third.todo) > 2:
        step((), *second, third)
    finish(*second)
    w_mo, w_ao = (chain.whole() for chain in second)
    gate_up = lax.all_gather(w_gate_up, ("dp", "seq"), axis=0, tiled=True)
    mamba_width = w_mamba_in.shape[1]
    w_z, w_x, w_q = w_in[:, :INNER], w_in[:, INNER:mamba_width], w_in[:, mamba_width:]

    smalls = w_q[:, QWIDTH + 2 * KWIDTH :]
    gain_one = smalls[:, MHEADS].astype(F32)
    gain_two = smalls[:, MHEADS + 1].astype(F32)
    at = MHEADS + 2
    conv_kernel = smalls[:, at : at + conv_cols].reshape(count, rows * conv_cols)[:, : taps_count * channels]
    conv_kernel = conv_kernel.reshape(count, taps_count, channels).transpose(1, 0, 2)
    conv_kernel = conv_kernel.reshape(taps_count, count * channels).astype(F32)
    at += conv_cols
    conv_shift = smalls[:, at : at + bias_cols].reshape(count, rows * bias_cols)[:, :channels]
    conv_shift = conv_shift.reshape(count * channels).astype(F32)

    length = tokens.shape[1]
    seg_full = segment_ids[0]
    total = seg_full.shape[0]
    rank = lax.axis_index("seq")
    first_row = rank * length
    back = taps_count - 1
    seg_padded = jnp.concatenate([jnp.full((back,), -1, jnp.int32), seg_full])
    seg_own = lax.dynamic_slice_in_dim(seg_full, first_row, length)
    seg_before = lax.dynamic_slice_in_dim(seg_padded, first_row + back - 1, 1)[0]
    taps = [
        (lax.dynamic_slice_in_dim(seg_padded, first_row + back - j, length) == seg_own).astype(F32)[:, None]
        for j in range(taps_count)
    ]
    seg_col = seg_own[:, None]
    seg_row = seg_own[None, :]
    rank_arg = rank.astype(jnp.int32).reshape(1)

    inputs = tokens[0].astype(F32)
    r1 = lax.rsqrt(jnp.mean(inputs * inputs, axis=-1, keepdims=True) + EPSILON)
    n1 = (inputs * r1 * gain_one[None, :]).astype(BF16)
    n1, w_mo, w_ao = step((n1, w_mo, w_ao), third)
    qkv_small = dot_nn(n1, w_q)
    qkv = qkv_small[:, : QWIDTH + 2 * KWIDTH]
    delta_raw = qkv_small[:, QWIDTH + 2 * KWIDTH : QWIDTH + 2 * KWIDTH + 128]
    xbc = dot_nn(n1, w_x).astype(BF16)
    z = dot_nn(n1, w_z).astype(BF16)


    freqs = ROPE_BASE ** (-(jnp.arange(AHDIM // 2).astype(F32) * 2.0 / AHDIM))
    angles = (first_row + jnp.arange(length, dtype=jnp.int32)).astype(F32)[:, None] * freqs[None, :]
    cosine = jnp.tile(jnp.cos(angles), (1, 4))
    sine_half = jnp.sin(angles)
    sine = jnp.tile(jnp.concatenate([-sine_half, sine_half], axis=1), (1, 2))
    q, keyvals = rope(qkv, cosine, sine)
    all_keyvals = gather_keyvals(keyvals)

    halo = jnp.pad(neighbour(xbc[length - back :], 1).astype(F32), ((8 - back, 0), (0, 0)))
    kernel_wide = jnp.concatenate([conv_kernel, conv_shift[None, :]])
    kernel_wide = jnp.pad(kernel_wide, ((0, 7 - taps_count), (0, 0)))
    taps_wide = jnp.pad(jnp.concatenate(taps, axis=1), ((0, 0), (0, 8 - taps_count)))
    u = conv_forward(xbc, halo, kernel_wide, taps_wide, taps_count)

    heads = jnp.stack([delta_bias, decay_log]).astype(F32)
    heads = jnp.pad(heads, ((0, 6), (0, 128 - MHEADS)))
    vec, row = heads_forward(seg_before.reshape(1), delta_raw, heads, seg_col)
    gate_lanes = jnp.repeat(vec[3, -1, :MHEADS], MHDIM)
    skip_lanes = jnp.repeat(skip_gain.astype(F32), MHDIM)[None, :]

    y_local, state_part = ssd_forward(u, u, u, vec, row, seg_col, seg_row)
    state_in = state_from_behind(gate_lanes, state_part)

    q, _ = tie(q, state_part)
    attended, lse = attend(rank_arg, q, all_keyvals, seg_col, seg_full.reshape(total // length, length))
    attended_low = attended.astype(BF16)

    y, mixed_low = ssd_finish(y_local, u, z, u, state_in, vec, skip_lanes)
    mixed_low = step(mixed_low, third)
    residual = inputs + dot_nn(mixed_low, w_mo) + dot_nn(attended_low, w_ao)

    r2 = lax.rsqrt(jnp.mean(residual * residual, axis=-1, keepdims=True) + EPSILON)
    n2 = (residual * r2 * gain_two[None, :]).astype(BF16)
    gu = dot_nn(n2, gate_up)
    gu = step(gu, third)
    down = third.whole()
    half = gu.shape[1] // 2
    gate, up = gu[:, :half], gu[:, half:]
    gate_act, gate_slope = silu_parts(gate)
    hidden = (gate_act * up).astype(BF16)
    upstream_low = cotangent[0]
    upstream = upstream_low.astype(F32)
    sum_down = Halving(dot_tn(hidden, upstream_low).astype(BF16), order_x)
    hidden = step(hidden, sum_down)
    block_out = (residual + dot_nn(hidden, down)).astype(BF16)
    upstream_low, block_out = step((upstream_low, block_out), sum_down)
    dhidden = dot_nt(upstream_low, down)
    dgate = (dhidden * up * gate_slope).astype(BF16)
    dup = (dhidden * gate_act).astype(BF16)
    dgu = jnp.concatenate([dgate, dup], axis=1)
    grad_gate_up = dot_tn(n2, dgu).astype(BF16)
    dgu, grad_gate_up = tie(dgu, grad_gate_up)
    grad_gate_up = lax.psum_scatter(grad_gate_up, ("dp", "seq"), scatter_dimension=0, tiled=True).astype(F32)
    dn2 = dot_nt(dgu, gate_up)
    scaled = gain_two[None, :] * dn2
    grad_gain_two = jnp.sum(dn2 * residual * r2, axis=0)
    dhs = upstream + r2 * scaled - residual * (r2 * r2 * r2) * jnp.mean(scaled * residual, axis=-1, keepdims=True)
    dhs_low = dhs.astype(BF16)
    dym = dot_nt(dhs_low, w_mo)
    do = dot_nt(dhs_low, w_ao).astype(BF16)
    sum_mo = Halving(dot_tn(mixed_low, dhs_low).astype(BF16), order_y)
    sum_ao = Halving(dot_tn(attended_low, dhs_low).astype(BF16), order_x)
    dym, do = step((dym, do), sum_mo, sum_ao)

    dy, dz, dstate_part, skip_cols = ssd_gate(dym, y, u, z, u, vec)
    dstate = state_from_ahead(gate_lanes, dstate_part)
    dz, dy = step((dz, dy), sum_down, sum_mo, sum_ao)
    sum_z = Halving(dot_tn(n1, dz).astype(BF16), order_y)
    dy = step(dy, sum_z)

    dx, db, dc, cols, rows_sum = ssd_backward(
        u, dy, u, u, state_in, dstate, vec, row, seg_row.T, seg_row, skip_lanes
    )
    cols, rows_sum, dx = step((cols, rows_sum, dx), sum_down, sum_ao, sum_mo, sum_z)
    ddelta_low, head_sums = heads_backward(delta_raw, heads, cols, rows_sum)
    grad_skip = jnp.sum(skip_cols.reshape(MHEADS, MHDIM), axis=1)
    sum_heads = Summing(jnp.concatenate([head_sums[0, :MHEADS], head_sums[1, :MHEADS], grad_skip]))

    dxbc, last_rows, spilled, conv_grads = conv_backward(dx, db, dc, xbc, halo, kernel_wide, taps_wide, taps_count)
    incoming = jnp.pad(neighbour(spilled[8 - back :], -1), ((8 - back, 0), (0, 0)))
    dxbc, last_rows = step((dxbc, last_rows), sum_down, sum_ao)
    dxbc = lax.dynamic_update_slice_in_dim(dxbc, (last_rows + incoming).astype(BF16), length - 8, 0)
    cut = 640
    sum_x = [
        Halving(dot_tn(n1, dxbc[:, :cut]).astype(BF16), order_y),
        Halving(dot_tn(n1, dxbc[:, cut : 2 * cut]).astype(BF16), order_x),
        Halving(dot_tn(n1, dxbc[:, 2 * cut :]).astype(BF16), order_x),
    ]
    do = step(do, *sum_x, sum_heads)

    owner = (jnp.arange(QWIDTH)[None, :] // AHDIM == jnp.arange(AHEADS)[:, None]).astype(F32)
    delta = lax.dot_general(
        owner, do.astype(F32) * attended, (((1,), (1,)), ((), ())), precision=lax.Precision.HIGHEST
    )
    do, delta = step((do, delta), *sum_x, sum_mo, sum_z)
    dq, dkv = attend_backward(
        rank_arg, q, all_keyvals, do, lse[:, :AHEADS].T, delta, seg_row, seg_full[:, None]
    )
    dq, dkv = step((dq, dkv), *sum_x, sum_heads, sum_z, sum_mo, sum_ao, sum_down)
    own_dkv, more_dkv = scatter_keyval_grads(dkv, length)
    dqkv = unrope(dq, own_dkv, more_dkv, cosine, sine)
    sum_qkv = Halving(dot_tn(n1, dqkv).astype(BF16), order_y)
    dqkv = step(dqkv, *sum_x, sum_heads, sum_z, sum_mo, sum_ao, sum_qkv)

    kernel_grad = conv_grads[:taps_count].reshape(taps_count, count, channels).transpose(1, 0, 2)
    kernel_grad = kernel_grad.reshape(count, taps_count * channels)
    shift_grad = conv_grads[taps_count].reshape(count, channels)
    def fit_all(value, columns):
        spare = rows * columns - value.shape[1]
        return jnp.pad(value, ((0, 0), (0, spare))).reshape(width, columns)

    ddelta_wide = jnp.pad(ddelta_low, ((0, 0), (0, small_width - 128)))
    dq_small = jnp.concatenate([dqkv, ddelta_wide], axis=1)
    dn1 = dot_nt(dq_small, w_q) + dot_nt(dz, w_z) + dot_nt(dxbc, w_x)
    scaled = gain_one[None, :] * dn1
    grad_gain_one = jnp.sum(dn1 * inputs * r1, axis=0)
    grad_tokens = dhs + r1 * scaled - inputs * (r1 * r1 * r1) * jnp.mean(scaled * inputs, axis=-1, keepdims=True)

    parts = [
        dot_tn(n1, ddelta_low)[:, :MHEADS],
        grad_gain_one[:, None],
        grad_gain_two[:, None],
        fit_all(kernel_grad, conv_cols),
        fit_all(shift_grad, bias_cols),
    ]
    used = sum(p.shape[1] for p in parts)
    parts.append(jnp.zeros((width, small_width - used), F32))
    small_sum = jnp.concatenate(parts, axis=1).astype(BF16).reshape(count, rows, small_width)
    small_sum = lax.all_to_all(small_sum, ("dp", "seq"), 0, 0, tiled=True)
    grad_small = jnp.sum(small_sum.astype(F32), axis=0)
    finish(sum_z, sum_qkv, sum_mo, sum_ao, sum_down, sum_heads, *sum_x)
    grad_x = jnp.concatenate([chain.value for chain in sum_x], axis=1)
    head_grads = sum_heads.value

    at = MHEADS + 2
    kernel_own = grad_small[:, at : at + conv_cols].reshape(-1)[: taps_count * channels].reshape(taps_count, channels)
    at += conv_cols
    shift_own = grad_small[:, at : at + bias_cols].reshape(-1)[:channels]
    return (
        block_out[None],
        grad_tokens[None],
        grad_small[:, MHEADS],
        jnp.concatenate([sum_z.value, grad_x], axis=1),
        grad_small[:, :MHEADS],
        kernel_own,
        shift_own,
        head_grads[:MHEADS],
        head_grads[MHEADS : 2 * MHEADS],
        head_grads[2 * MHEADS :],
        sum_mo.value,
        sum_qkv.value,
        sum_ao.value,
        grad_small[:, MHEADS + 1],
        grad_gate_up,
        sum_down.value,
    )


def solution(mesh):
    both = ("dp", "seq")
    in_specs = (
        P("dp", "seq", None),
        P("dp", None),
        P(both),
        P(both, None),
        P(both, None),
        P(None, both),
        P(both),
        P(),
        P(),
        P(),
        P(both, None),
        P(both, None),
        P(both, None),
        P(both),
        P(both, None),
        P(both, None),
        P("dp", "seq", None),
    )
    out_specs = (
        P("dp", "seq", None),
        P("dp", "seq", None),
        P(both),
        P(both, None),
        P(both, None),
        P(None, both),
        P(both),
        P(),
        P(),
        P(),
        P(both, None),
        P(both, None),
        P(both, None),
        P(both),
        P(both, None),
        P(both, None),
    )
    return jax.shard_map(
        on_device, mesh=mesh, in_specs=in_specs, out_specs=out_specs, check_vma=False
    )
```

```python
import math
from functools import partial

import jax
import jax.numpy as jnp
from jax import lax
from jax.experimental import pallas as pl
from jax.experimental.pallas import tpu as pltpu
from jax.sharding import PartitionSpec as P

MHEADS = 24
MHDIM = 64
STATE = 128
AHEADS = 8
KVHEADS = 2
AHDIM = 64

INNER = MHEADS * MHDIM
CONVD = INNER + 2 * STATE
QWIDTH = AHEADS * AHDIM
KWIDTH = KVHEADS * AHDIM
GROUPS = 3
GHEADS = MHEADS // GROUPS
GLANES = GHEADS * MHDIM
STRIP = 128

EPSILON = 1e-05
ROPE_BASE = 100000000000.0
NEGATIVE = -1e30
LOG2E = math.log2(math.e)

F32 = jnp.float32
BF16 = jnp.bfloat16


def dot_nn(a, b):
    return lax.dot_general(a, b, (((1,), (0,)), ((), ())), preferred_element_type=F32)


def dot_nt(a, b):
    return lax.dot_general(a, b, (((1,), (1,)), ((), ())), preferred_element_type=F32)


def dot_tn(a, b):
    return lax.dot_general(a, b, (((0,), (0,)), ((), ())), preferred_element_type=F32)


def mesh_bits():
    bits = []
    for axis in ("dp", "seq"):
        size = lax.axis_size(axis)
        level = size // 2
        while level:
            bits.append((axis, level))
            level //= 2
    return bits


def bit_orders():
    bits = mesh_bits()
    seq = [b for b in bits if b[0] == "seq"][::-1]
    dp = [b for b in bits if b[0] == "dp"][::-1]
    pair, second, rest = dp[:1], dp[1:2], dp[2:]
    return pair + seq + second + rest, pair + second + seq + rest


def swap(value, bit):
    axis, level = bit
    size = lax.axis_size(axis)
    return lax.ppermute(value, axis, [(i, i ^ level) for i in range(size)])


def bit_here(bit):
    axis, level = bit
    return (lax.axis_index(axis) // level) % 2


def tie(values, arrays):
    return lax.optimization_barrier((values, arrays))


class Halving:
    def __init__(self, full, order):
        self.left = mesh_bits()
        rows = full.shape[0] >> len(self.left)
        self.value = full.reshape((2,) * len(self.left) + (rows, full.shape[1]))
        self.todo = list(order)
        self.bit = self.out = self.got = None

    def prepare(self):
        if self.got is not None:
            place = self.left.index(self.bit)
            kept = lax.dynamic_index_in_dim(self.value, bit_here(self.bit), place, keepdims=False)
            self.left.remove(self.bit)
            value = kept.astype(F32) + self.got.astype(F32)
            self.value = value.astype(BF16) if self.left else value
            self.got = self.out = None
        if self.todo:
            self.bit = self.todo.pop(0)
            place = self.left.index(self.bit)
            self.out = lax.dynamic_index_in_dim(self.value, 1 - bit_here(self.bit), place, keepdims=False)

    def arrays(self):
        return (self.value,) if self.out is None else (self.value, self.out)

    def launch(self, arrays):
        self.value = arrays[0]
        if self.out is not None:
            self.out = arrays[1]
            self.got = swap(self.out, self.bit)


class Doubling:
    def __init__(self, shard, order):
        self.rows, self.columns = shard.shape
        self.value = shard
        self.todo = list(reversed(order))
        self.held = []
        self.bit = self.got = None

    def prepare(self):
        if self.got is not None:
            here = bit_here(self.bit)
            self.held = [b for b in mesh_bits() if b in self.held or b == self.bit]
            place = self.held.index(self.bit)
            own = (jnp.arange(2) == here).reshape((2,) + (1,) * (self.value.ndim - place))
            self.value = jnp.where(own, jnp.expand_dims(self.value, place), jnp.expand_dims(self.got, place))
            self.got = None
        self.bit = self.todo.pop(0) if self.todo else None

    def arrays(self):
        return (self.value,)

    def launch(self, arrays):
        (self.value,) = arrays
        if self.bit is not None:
            self.got = swap(self.value, self.bit)

    def whole(self):
        return self.value.reshape((self.rows << len(self.held), self.columns))


class Summing:
    def __init__(self, value):
        self.value = value
        self.todo = mesh_bits()
        self.bit = self.got = None

    def prepare(self):
        if self.got is not None:
            self.value = self.value + self.got
            self.got = None
        self.bit = self.todo.pop(0) if self.todo else None

    def arrays(self):
        return (self.value,)

    def launch(self, arrays):
        (self.value,) = arrays
        if self.bit is not None:
            self.got = swap(self.value, self.bit)


def step(values, *chains):
    for chain in chains:
        chain.prepare()
    values, arrays = tie(values, [chain.arrays() for chain in chains])
    for chain, own in zip(chains, arrays):
        chain.launch(own)
    return values


def finish(*chains):
    while any(chain.todo or chain.got is not None for chain in chains):
        step((), *chains)


def compose_maps(earlier, later):
    return (later[0] * earlier[0], later[0][None, :] * earlier[1] + later[1])


def state_from_behind(gate, part):
    count = lax.axis_size("seq")
    low = part.astype(BF16)
    if count == 2:
        return lax.ppermute(low, "seq", [(0, 1)])
    gates = lax.all_gather(gate.astype(BF16), "seq")
    parts = lax.all_gather(low, "seq")
    start = (jnp.ones_like(gate), jnp.zeros_like(part))

    def one(step, state):
        return compose_maps(
            state,
            (
                lax.dynamic_index_in_dim(gates, step, 0, False).astype(F32),
                lax.dynamic_index_in_dim(parts, step, 0, False).astype(F32),
            ),
        )

    return lax.fori_loop(0, lax.axis_index("seq"), one, start)[1]


def state_from_ahead(gate, part):
    count = lax.axis_size("seq")
    low = part.astype(BF16)
    if count == 2:
        return lax.ppermute(low, "seq", [(1, 0)])
    gates = lax.all_gather(gate.astype(BF16), "seq")
    parts = lax.all_gather(low, "seq")
    start = (jnp.ones_like(gate), jnp.zeros_like(part))
    place = lax.axis_index("seq")

    def one(step, state):
        at = count - 1 - step
        return compose_maps(
            state,
            (
                lax.dynamic_index_in_dim(gates, at, 0, False).astype(F32),
                lax.dynamic_index_in_dim(parts, at, 0, False).astype(F32),
            ),
        )

    return lax.fori_loop(0, count - 1 - place, one, start)[1]


def neighbour(value, steps):
    count = lax.axis_size("seq")
    first, last = (max(0, -steps), min(count, count - steps))
    return lax.ppermute(value, "seq", [(s, s + steps) for s in range(first, last)])


SHORT = pl.CostEstimate(flops=0, bytes_accessed=0, transcendentals=0)
PARAMS = pltpu.CompilerParams(vmem_limit_bytes=48 * 1024 * 1024)


def group_columns(vec_ref, which):
    shift = lax.rem(128 - pl.program_id(0) * GHEADS, 128)
    return pltpu.roll(vec_ref[which], shift, 1)


def lane_is_low(rows):
    return lax.broadcasted_iota(jnp.int32, (rows, 128), 1) < MHDIM


def spread(low, vec, head):
    return jnp.where(low, vec[:, head : head + 1], vec[:, head + 1 : head + 2])


def ssd_forward_kernel(x_ref, b_ref, c_ref, vec_ref, row_ref, segc_ref, segr_ref, y_ref, st_ref, cb_ref, cum_ref):
    length = x_ref.shape[0]

    @pl.when(pl.program_id(0) == 0)
    def _():
        t = lax.broadcasted_iota(jnp.int32, (length, length), 0)
        s = lax.broadcasted_iota(jnp.int32, (length, length), 1)
        seen = (t >= s) & (segc_ref[...] == segr_ref[...])
        cb = dot_nt(c_ref[...].astype(BF16), b_ref[...].astype(BF16))
        cb_ref[...] = jnp.where(seen, cb, 0.0)

    b_low = b_ref[...].astype(BF16)
    wide = lane_is_low(length)
    narrow = lane_is_low(STRIP)
    dt = group_columns(vec_ref, 0)
    rem = group_columns(vec_ref, 2)
    cum_ref[...] = group_columns(vec_ref, 1)
    for pair in range(GHEADS // 2):
        lanes = slice(pair * 128, (pair + 1) * 128)
        xd = x_ref[:, lanes] * spread(wide, dt, 2 * pair)
        xd_low = xd.astype(BF16)
        st_ref[:, lanes] = dot_tn(b_low, (xd * spread(wide, rem, 2 * pair)).astype(BF16))
        for strip in range(length // STRIP):
            first, width = strip * STRIP, (strip + 1) * STRIP
            halves = []
            for head in (2 * pair, 2 * pair + 1):
                gap = cum_ref[first : first + STRIP, head : head + 1] - row_ref[head : head + 1, :width]
                decay = jnp.exp2(jnp.minimum(gap, 0.0))
                m = (decay * cb_ref[first : first + STRIP, :width]).astype(BF16)
                halves.append(dot_nn(m, xd_low[:width]))
            y_ref[first : first + STRIP, lanes] = jnp.where(narrow, halves[0], halves[1])


def group_specs(length):
    x_spec = pl.BlockSpec((length, GLANES), lambda g: (0, g))
    s_spec = pl.BlockSpec((STATE, GLANES), lambda g: (0, g))
    n_spec = pl.BlockSpec((length, STATE), lambda g: (0, 0))
    b_spec = pl.BlockSpec((length, STATE), lambda g: (0, INNER // STATE))
    c_spec = pl.BlockSpec((length, STATE), lambda g: (0, INNER // STATE + 1))
    v_spec = pl.BlockSpec((4, length, 128), lambda g: (0, 0, 0))
    r_spec = pl.BlockSpec((GHEADS, length), lambda g: (g, 0))
    return x_spec, s_spec, n_spec, b_spec, c_spec, v_spec, r_spec


def ssd_forward(x, b, c, vec, row, seg_col, seg_row):
    length = x.shape[0]
    x_spec, s_spec, n_spec, b_spec, c_spec, v_spec, r_spec = group_specs(length)
    return pl.pallas_call(
        ssd_forward_kernel,
        grid=(GROUPS,),
        in_specs=[
            x_spec, b_spec, c_spec, v_spec, r_spec,
            pl.BlockSpec((length, 1), lambda g: (0, 0)),
            pl.BlockSpec((1, length), lambda g: (0, 0)),
        ],
        out_specs=[x_spec, s_spec],
        out_shape=[
            jax.ShapeDtypeStruct((length, INNER), F32),
            jax.ShapeDtypeStruct((STATE, INNER), F32),
        ],
        scratch_shapes=[pltpu.VMEM((length, length), F32), pltpu.VMEM((length, 128), F32)],
        compiler_params=PARAMS,
        cost_estimate=SHORT,
        name="ssd_forward",
    )(x, b, c, vec, row, seg_col, seg_row)


def silu_parts(v):
    sig = 1.0 / (1.0 + jnp.exp(-v))
    return v * sig, sig * (1.0 + v * (1.0 - sig))


def ssd_finish_kernel(y0_ref, x_ref, z_ref, c_ref, st_ref, vec_ref, skip_ref, y_ref, ym_ref):
    length = x_ref.shape[0]
    wide = lane_is_low(length)
    ent = group_columns(vec_ref, 3)
    c_low = c_ref[...].astype(BF16)
    for pair in range(GHEADS // 2):
        lanes = slice(pair * 128, (pair + 1) * 128)
        cs = dot_nn(c_low, st_ref[:, lanes].astype(BF16))
        y = y0_ref[:, lanes] + spread(wide, ent, 2 * pair) * cs + skip_ref[:, lanes] * x_ref[:, lanes]
        gate, _ = silu_parts(z_ref[:, lanes].astype(F32))
        y_ref[:, lanes] = y
        ym_ref[:, lanes] = (y * gate).astype(BF16)


def ssd_finish(y0, x, z, c, state, vec, skip):
    length = x.shape[0]
    x_spec, s_spec, n_spec, b_spec, c_spec, v_spec, _ = group_specs(length)
    return pl.pallas_call(
        ssd_finish_kernel,
        grid=(GROUPS,),
        in_specs=[x_spec, x_spec, x_spec, c_spec, s_spec, v_spec, pl.BlockSpec((1, GLANES), lambda g: (0, g))],
        out_specs=[x_spec, x_spec],
        out_shape=[
            jax.ShapeDtypeStruct((length, INNER), F32),
            jax.ShapeDtypeStruct((length, INNER), BF16),
        ],
        compiler_params=PARAMS,
        cost_estimate=SHORT,
        name="ssd_finish",
    )(y0, x, z, c, state, vec, skip)


def ssd_gate_kernel(dym_ref, y_ref, x_ref, z_ref, c_ref, vec_ref, dy_ref, dz_ref, ds_ref, skip_ref):
    length = x_ref.shape[0]
    spot = lax.broadcasted_iota(jnp.int32, (128, 128), 0) // MHDIM
    place = lax.broadcasted_iota(jnp.int32, (128, 128), 1)

    @pl.when(pl.program_id(0) == 0)
    def _():
        skip_ref[...] = jnp.zeros_like(skip_ref)

    wide = lane_is_low(length)
    ent = group_columns(vec_ref, 3)
    c_low = c_ref[...].astype(BF16)
    for pair in range(GHEADS // 2):
        lanes = slice(pair * 128, (pair + 1) * 128)
        gate, slope = silu_parts(z_ref[:, lanes].astype(F32))
        dym = dym_ref[:, lanes]
        dy = dym * gate
        dy_ref[:, lanes] = dy
        dz_ref[:, lanes] = (dym * y_ref[:, lanes] * slope).astype(BF16)
        ds_ref[:, lanes] = dot_tn(c_low, (dy * spread(wide, ent, 2 * pair)).astype(BF16))
        total = jnp.broadcast_to(jnp.sum(dy * x_ref[:, lanes], axis=0, keepdims=True), (8, 128))
        pick = (place == pl.program_id(0) * GHEADS + 2 * pair + spot).astype(BF16)
        high = total.astype(BF16)
        rest = (total - high.astype(F32)).astype(BF16)
        skip_ref[...] += dot_nn(high, pick) + dot_nn(rest, pick)


def ssd_gate(dym, y, x, z, c, vec):
    length = x.shape[0]
    x_spec, s_spec, n_spec, b_spec, c_spec, v_spec, _ = group_specs(length)
    one_spec = pl.BlockSpec((8, 128), lambda g: (0, 0))
    return pl.pallas_call(
        ssd_gate_kernel,
        grid=(GROUPS,),
        in_specs=[x_spec, x_spec, x_spec, x_spec, c_spec, v_spec],
        out_specs=[x_spec, x_spec, s_spec, one_spec],
        out_shape=[
            jax.ShapeDtypeStruct((length, INNER), F32),
            jax.ShapeDtypeStruct((length, INNER), BF16),
            jax.ShapeDtypeStruct((STATE, INNER), F32),
            jax.ShapeDtypeStruct((8, 128), F32),
        ],
        compiler_params=PARAMS,
        cost_estimate=SHORT,
        name="ssd_gate",
    )(dym, y, x, z, c, vec)


def ssd_backward_kernel(
    x_ref, dy_ref, b_ref, c_ref, st_ref, dst_ref, vec_ref, row_ref, segc_ref, segr_ref, skip_ref,
    dx_ref, db_ref, dc_ref, cols_ref, rows_ref, bc_ref, dbc_ref, xd_ref, sum_ref, cum_ref,
):
    length = x_ref.shape[0]
    group = pl.program_id(0)

    @pl.when(group == 0)
    def _():
        s = lax.broadcasted_iota(jnp.int32, (length, length), 0)
        t = lax.broadcasted_iota(jnp.int32, (length, length), 1)
        seen = (t >= s) & (segc_ref[...] == segr_ref[...])
        bc = dot_nt(b_ref[...].astype(BF16), c_ref[...].astype(BF16))
        bc_ref[...] = jnp.where(seen, bc, 0.0)
        dbc_ref[...] = jnp.zeros_like(dbc_ref)
        db_ref[...] = jnp.zeros_like(db_ref)
        dc_ref[...] = jnp.zeros_like(dc_ref)
        cols_ref[...] = jnp.zeros_like(cols_ref)

    b_low = b_ref[...].astype(BF16)
    c_low = c_ref[...].astype(BF16)
    wide = lane_is_low(length)
    narrow = lane_is_low(STRIP)
    lane = lax.broadcasted_iota(jnp.int32, (STRIP, 128), 1)
    spot = lax.broadcasted_iota(jnp.int32, (128, 128), 0) // MHDIM
    place = lax.broadcasted_iota(jnp.int32, (128, 128), 1)
    dt = group_columns(vec_ref, 0)
    rem = group_columns(vec_ref, 2)
    ent = group_columns(vec_ref, 3)
    cum_ref[...] = group_columns(vec_ref, 1)
    rows_ref[...] = jnp.zeros_like(rows_ref)
    for pair in range(GHEADS // 2):
        lanes = slice(pair * 128, (pair + 1) * 128)
        x = x_ref[:, lanes]
        dy = dy_ref[:, lanes]
        dtx = spread(wide, dt, 2 * pair)
        remx = spread(wide, rem, 2 * pair)
        entx = spread(wide, ent, 2 * pair)
        dy_low = dy.astype(BF16)
        xd_ref[...] = (x * dtx).astype(BF16)
        st_low = st_ref[:, lanes].astype(BF16)
        dst_low = dst_ref[:, lanes].astype(BF16)
        carried = remx * dot_nn(b_low, dst_low)
        entered = entx * dot_nn(c_low, st_low)
        dc_ref[...] += dot_nt((entx * dy).astype(BF16), st_low)
        db_ref[...] += dot_nt((dtx * remx * x).astype(BF16), dst_low)
        for strip in range(length // STRIP):
            first = strip * STRIP
            xd = xd_ref[first : first + STRIP, :]
            dys = dy_low[first:]
            halves = []
            dgs = []
            gones = []
            for half in range(2):
                head = 2 * pair + half
                mine = narrow if half == 0 else ~narrow
                gap = row_ref[head : head + 1, first:] - cum_ref[first : first + STRIP, head : head + 1]
                decay = jnp.exp2(jnp.minimum(gap, 0.0))
                bc = bc_ref[first : first + STRIP, first:]
                m = (decay * bc).astype(BF16)
                halves.append(dot_nn(m, dys))
                dg = decay * dot_nt(jnp.where(mine, xd, jnp.zeros_like(xd)), dys)
                dgs.append(dg)
                e = dg * bc
                rows_ref[head : head + 1, first:] += jnp.sum(e, axis=0, keepdims=True)
                gones.append(jnp.sum(e, axis=1, keepdims=True))
            dbc_ref[first : first + STRIP, first:] += dgs[0] + dgs[1]
            at = group * GHEADS + 2 * pair
            cols_ref[3, first : first + STRIP, :] += jnp.where(
                lane == at, gones[0], jnp.where(lane == at + 1, gones[1], 0.0)
            )
            dxd = jnp.where(narrow, halves[0], halves[1]) + carried[first : first + STRIP]
            sum_ref[first : first + STRIP, :] = dxd
        dxd = sum_ref[...]
        dx_ref[:, lanes] = dtx * dxd + skip_ref[:, lanes] * dy
        pick = (place == group * GHEADS + 2 * pair + spot).astype(BF16)

        def per_head(value):
            high = value.astype(BF16)
            rest = (value - high.astype(F32)).astype(BF16)
            return dot_nn(high, pick) + dot_nn(rest, pick)

        cols_ref[0] += per_head(dxd * x)
        cols_ref[1] += per_head(dtx * x * carried)
        cols_ref[2] += per_head(dy * entered)
        passed = jnp.sum(st_ref[:, lanes].astype(F32) * dst_ref[:, lanes].astype(F32), axis=0, keepdims=True) * entx[length - 1 :]
        cols_ref[2, length - 8 :, :] += jnp.where(
            lax.broadcasted_iota(jnp.int32, (8, 128), 0) == 7, per_head(jnp.broadcast_to(passed, (8, 128))), 0.0
        )

    @pl.when(group == GROUPS - 1)
    def _():
        s = lax.broadcasted_iota(jnp.int32, (length, length), 0)
        t = lax.broadcasted_iota(jnp.int32, (length, length), 1)
        seen = (t >= s) & (segc_ref[...] == segr_ref[...])
        dbc = jnp.where(seen, dbc_ref[...], 0.0).astype(BF16)
        db_ref[...] += dot_nn(dbc, c_low)
        dc_ref[...] += dot_tn(dbc, b_low)


def ssd_backward(x, dy, b, c, state, dstate, vec, row, seg_col, seg_row, skip):
    length = x.shape[0]
    x_spec, s_spec, n_spec, b_spec, c_spec, v_spec, r_spec = group_specs(length)
    return pl.pallas_call(
        ssd_backward_kernel,
        grid=(GROUPS,),
        in_specs=[
            x_spec, x_spec, b_spec, c_spec, s_spec, s_spec, v_spec, r_spec,
            pl.BlockSpec((length, 1), lambda g: (0, 0)),
            pl.BlockSpec((1, length), lambda g: (0, 0)),
            pl.BlockSpec((1, GLANES), lambda g: (0, g)),
        ],
        out_specs=[x_spec, n_spec, n_spec, pl.BlockSpec((4, length, 128), lambda g: (0, 0, 0)), r_spec],
        out_shape=[
            jax.ShapeDtypeStruct((length, INNER), F32),
            jax.ShapeDtypeStruct((length, STATE), F32),
            jax.ShapeDtypeStruct((length, STATE), F32),
            jax.ShapeDtypeStruct((4, length, 128), F32),
            jax.ShapeDtypeStruct((MHEADS, length), F32),
        ],
        scratch_shapes=[
            pltpu.VMEM((length, length), F32),
            pltpu.VMEM((length, length), F32),
            pltpu.VMEM((length, 128), BF16),
            pltpu.VMEM((length, 128), F32),
            pltpu.VMEM((length, 128), F32),
        ],
        compiler_params=PARAMS,
        cost_estimate=SHORT,
        name="ssd_backward",
    )(x, dy, b, c, state, dstate, vec, row, seg_col, seg_row, skip)


def conv_of(ext_ref, kernel_ref, taps_ref, taps_count):
    length = taps_ref.shape[0]
    total = jnp.zeros((length, ext_ref.shape[1]), F32) + kernel_ref[taps_count : taps_count + 1, :]
    for j in range(taps_count):
        total = total + kernel_ref[j : j + 1, :] * ext_ref[8 - j : 8 - j + length, :] * taps_ref[:, j : j + 1]
    return total


def conv_kernel_body(taps_count, xbc_ref, halo_ref, kernel_ref, taps_ref, u_ref, ext_ref):
    ext_ref[:8, :] = halo_ref[...]
    ext_ref[8:, :] = xbc_ref[...].astype(F32)
    xc = conv_of(ext_ref, kernel_ref, taps_ref, taps_count)
    u_ref[...] = silu_parts(xc)[0]


def conv_forward(xbc, halo, kernel, taps, taps_count):
    length, channels = xbc.shape
    wide = 256
    spec = pl.BlockSpec((length, wide), lambda g: (0, g))
    eight = pl.BlockSpec((8, wide), lambda g: (0, g))
    return pl.pallas_call(
        partial(conv_kernel_body, taps_count),
        grid=(channels // wide,),
        in_specs=[spec, eight, eight, pl.BlockSpec((length, 8), lambda g: (0, 0))],
        out_specs=spec,
        out_shape=jax.ShapeDtypeStruct((length, channels), F32),
        scratch_shapes=[pltpu.VMEM((length + 8, wide), F32)],
        compiler_params=PARAMS,
        cost_estimate=SHORT,
        name="conv_forward",
    )(xbc, halo, kernel, taps)


def conv_backward_body(
    taps_count, dx_ref, db_ref, dc_ref, xbc_ref, halo_ref, kernel_ref, taps_ref,
    out_ref, last_ref, spill_ref, grad_ref, ext_ref, du_ref, put_ref, mask_ref,
):
    length = taps_ref.shape[0]
    block = pl.program_id(0)
    heads_blocks = INNER // 128

    @pl.when(block == 0)
    def _():
        for j in range(taps_count):
            mask_ref[j] = jnp.broadcast_to(taps_ref[:, j : j + 1], (length, 128))

    @pl.when(block < heads_blocks)
    def _():
        du_ref[...] = dx_ref[...]

    @pl.when(block == heads_blocks)
    def _():
        du_ref[...] = db_ref[...]

    @pl.when(block == heads_blocks + 1)
    def _():
        du_ref[...] = dc_ref[...]

    ext_ref[:8, :] = halo_ref[...]
    ext_ref[8:, :] = xbc_ref[...].astype(F32)
    xc = jnp.zeros((length, 128), F32) + kernel_ref[taps_count : taps_count + 1, :]
    for j in range(taps_count):
        xc = xc + kernel_ref[j : j + 1, :] * ext_ref[8 - j : 8 - j + length, :] * mask_ref[j]
    dxc = du_ref[...] * silu_parts(xc)[1]
    put_ref[:8, :] = jnp.zeros((8, 128), F32)
    put_ref[8 + length :, :] = jnp.zeros((8, 128), F32)
    total = jnp.zeros((length + 8, 128), F32)
    sums = []
    for j in range(taps_count):
        masked = dxc * mask_ref[j]
        sums.append(jnp.sum(masked * ext_ref[8 - j : 8 - j + length, :], axis=0, keepdims=True))
        put_ref[8 : 8 + length, :] = masked * kernel_ref[j : j + 1, :]
        total = total + put_ref[j : j + length + 8, :]
    sums.append(jnp.sum(dxc, axis=0, keepdims=True))
    sums.append(jnp.zeros((7 - taps_count, 128), F32))
    spill_ref[...] = total[:8]
    out_ref[...] = total[8:].astype(BF16)
    last_ref[...] = total[length:]
    grad_ref[...] = jnp.concatenate(sums, axis=0)


def conv_backward(dx, db, dc, xbc, halo, kernel, taps, taps_count):
    length, channels = xbc.shape
    last = INNER // 128 - 1
    spec = pl.BlockSpec((length, 128), lambda g: (0, g))
    whole = pl.BlockSpec((length, 128), lambda g: (0, 0))
    eight = pl.BlockSpec((8, 128), lambda g: (0, g))
    return pl.pallas_call(
        partial(conv_backward_body, taps_count),
        grid=(channels // 128,),
        in_specs=[
            pl.BlockSpec((length, 128), lambda g: (0, jnp.minimum(g, last))), whole, whole,
            spec, eight, eight, pl.BlockSpec((length, 8), lambda g: (0, 0)),
        ],
        out_specs=[spec, eight, eight, eight],
        out_shape=[
            jax.ShapeDtypeStruct((length, channels), BF16),
            jax.ShapeDtypeStruct((8, channels), F32),
            jax.ShapeDtypeStruct((8, channels), F32),
            jax.ShapeDtypeStruct((8, channels), F32),
        ],
        scratch_shapes=[
            pltpu.VMEM((length + 8, 128), F32),
            pltpu.VMEM((length, 128), F32),
            pltpu.VMEM((length + 16, 128), F32),
            pltpu.VMEM((taps_count, length, 128), F32),
        ],
        compiler_params=PARAMS,
        cost_estimate=SHORT,
        name="conv_backward",
    )(dx, db, dc, xbc, halo, kernel, taps)


def softplus(v):
    return jnp.maximum(v, 0.0) + jnp.log1p(jnp.exp(-jnp.abs(v)))


def exact_dot(a, b):
    return lax.dot_general(
        a, b, (((1,), (0,)), ((), ())), precision=lax.Precision.HIGHEST, preferred_element_type=F32
    )


def head_values(raw_ref, heads_ref):
    real = lax.broadcasted_iota(jnp.int32, raw_ref.shape, 1) < MHEADS
    shifted = jnp.where(real, raw_ref[...] + heads_ref[0:1, :], 0.0)
    dt = jnp.where(real, softplus(shifted), 0.0)
    rate = jnp.exp(heads_ref[1:2, :])
    return shifted, dt, rate, -dt * rate


def heads_kernel(before_ref, raw_ref, heads_ref, seg_ref, vec_ref, row_ref):
    length = raw_ref.shape[0]
    _, dt, _, log_decay = head_values(raw_ref, heads_ref)
    t = lax.broadcasted_iota(jnp.int32, (length, length), 0)
    s = lax.broadcasted_iota(jnp.int32, (length, length), 1)
    cumulative = exact_dot(jnp.where(t >= s, 1.0, 0.0), log_decay)
    final = cumulative[length - 1 :]
    seg = seg_ref[...]
    vec_ref[0] = dt
    vec_ref[1] = cumulative * LOG2E
    vec_ref[2] = jnp.where(seg == seg[length - 1 :], jnp.exp(final - cumulative), 0.0)
    vec_ref[3] = jnp.where(seg == before_ref[0], jnp.exp(cumulative), 0.0)
    row_ref[...] = (cumulative * LOG2E).T


def heads_forward(before, raw, heads, seg_col):
    length = raw.shape[0]
    vmem = pl.BlockSpec(memory_space=pltpu.VMEM)
    return pl.pallas_call(
        heads_kernel,
        in_specs=[pl.BlockSpec(memory_space=pltpu.SMEM)] + [vmem] * 3,
        out_specs=[vmem, vmem],
        out_shape=[
            jax.ShapeDtypeStruct((4, length, 128), F32),
            jax.ShapeDtypeStruct((128, length), F32),
        ],
        compiler_params=PARAMS,
        cost_estimate=SHORT,
        name="heads_forward",
    )(before, raw, heads, seg_col)


def heads_backward_kernel(raw_ref, heads_ref, cols_ref, rows_ref, skip_ref, low_ref, sums_ref):
    length = raw_ref.shape[0]
    shifted, _, rate, log_decay = head_values(raw_ref, heads_ref)
    filler = jnp.zeros((128 - MHEADS, length), F32)
    gained = jnp.concatenate([rows_ref[...], filler], axis=0).T
    leaving = cols_ref[1]
    change = gained - cols_ref[3] + cols_ref[2] - leaving
    t = lax.broadcasted_iota(jnp.int32, (length, length), 0)
    s = lax.broadcasted_iota(jnp.int32, (length, length), 1)
    da = exact_dot(jnp.where(t <= s, 1.0, 0.0), change) + jnp.sum(leaving, axis=0, keepdims=True)
    real = lax.broadcasted_iota(jnp.int32, raw_ref.shape, 1) < MHEADS
    ddelta = jnp.where(real, (cols_ref[0] - da * rate) / (1.0 + jnp.exp(-shifted)), 0.0)
    low_ref[...] = ddelta.astype(BF16)
    sums_ref[...] = jnp.concatenate(
        [
            jnp.sum(ddelta, axis=0, keepdims=True),
            jnp.sum(da * log_decay, axis=0, keepdims=True),
            skip_ref[0:1, :],
            jnp.zeros((5, 128), F32),
        ],
        axis=0,
    )


def heads_backward(raw, heads, cols, rows, skip):
    length = raw.shape[0]
    return pl.pallas_call(
        heads_backward_kernel,
        out_shape=[
            jax.ShapeDtypeStruct((length, 128), BF16),
            jax.ShapeDtypeStruct((8, 128), F32),
        ],
        compiler_params=PARAMS,
        cost_estimate=SHORT,
        name="heads_backward",
    )(raw, heads, cols, rows, skip)


def turn(value, cosine, sine):
    low = (lax.broadcasted_iota(jnp.int32, value.shape, 1) % AHDIM) < AHDIM // 2
    other = jnp.where(low, pltpu.roll(value, 128 - AHDIM // 2, 1), pltpu.roll(value, AHDIM // 2, 1))
    return value * cosine + other * sine


def rope_kernel(qkv_ref, cos_ref, sin_ref, q_ref, kv_ref):
    cosine, sine = cos_ref[...], sin_ref[...]
    scale = AHDIM ** (-0.5)
    for at in range(QWIDTH // 128):
        lanes = slice(at * 128, (at + 1) * 128)
        q_ref[:, lanes] = (turn(qkv_ref[:, lanes], cosine, sine).astype(BF16).astype(F32) * scale).astype(BF16)
    kv_ref[:, :KWIDTH] = turn(qkv_ref[:, QWIDTH : QWIDTH + KWIDTH], cosine, sine).astype(BF16)
    kv_ref[:, KWIDTH:] = qkv_ref[:, QWIDTH + KWIDTH :].astype(BF16)


def rope(qkv, cosine, sine):
    length = qkv.shape[0]
    return pl.pallas_call(
        rope_kernel,
        out_shape=[
            jax.ShapeDtypeStruct((length, QWIDTH), BF16),
            jax.ShapeDtypeStruct((length, 2 * KWIDTH), BF16),
        ],
        compiler_params=PARAMS,
        cost_estimate=SHORT,
        name="rope",
    )(qkv, cosine, sine)


def unrope_kernel(dq_ref, dkv_ref, more_ref, cos_ref, sin_ref, out_ref):
    cosine, sine = cos_ref[...], -sin_ref[...]
    scale = AHDIM ** (-0.5)
    for at in range(QWIDTH // 128):
        lanes = slice(at * 128, (at + 1) * 128)
        out_ref[:, lanes] = (turn(dq_ref[:, lanes], cosine, sine) * scale).astype(BF16)
    dkv = dkv_ref[...] + more_ref[...].astype(F32)
    out_ref[:, QWIDTH : QWIDTH + KWIDTH] = turn(dkv[:, :KWIDTH], cosine, sine).astype(BF16)
    out_ref[:, QWIDTH + KWIDTH :] = dkv[:, KWIDTH:].astype(BF16)


def unrope(dq, dkv, more, cosine, sine):
    length = dq.shape[0]
    return pl.pallas_call(
        unrope_kernel,
        out_shape=jax.ShapeDtypeStruct((length, QWIDTH + 2 * KWIDTH), BF16),
        compiler_params=PARAMS,
        cost_estimate=SHORT,
        name="unrope",
    )(dq, dkv, more, cosine, sine)


def repeat_heads(kv_ref, k_ref, v_ref):
    low = lane_is_low(kv_ref.shape[0])
    for start, out in ((0, k_ref), (KWIDTH, v_ref)):
        own = kv_ref[:, start : start + KWIDTH].astype(F32)
        moved = pltpu.roll(own, AHDIM, 1)
        out[0] = jnp.where(low, own, moved).astype(BF16)
        out[1] = jnp.where(low, moved, own).astype(BF16)


def attend_kernel(rank_ref, q_ref, kv_ref, segq_ref, segk_ref, o_ref, lse_ref, top_ref, sum_ref, acc_ref, mask_ref, k_ref, v_ref):
    length = q_ref.shape[0]
    repeat_heads(kv_ref, k_ref, v_ref)
    rank = rank_ref[0]
    top_ref[...] = jnp.full_like(top_ref, NEGATIVE)
    sum_ref[...] = jnp.zeros_like(sum_ref)
    acc_ref[...] = jnp.zeros_like(acc_ref)
    narrow = lane_is_low(STRIP)

    def block(step, carry, diagonal=False):
        at = rank - step
        t = lax.broadcasted_iota(jnp.int32, (length, length), 0) + rank * length
        s = lax.broadcasted_iota(jnp.int32, (length, length), 1) + at * length
        seen = (s <= t) & (segq_ref[...] == segk_ref[pl.ds(at, 1), :])
        mask_ref[...] = jnp.where(seen, 0.0, NEGATIVE)
        start = pl.multiple_of(at * length, length)
        for head in range(AHEADS):
            kv_head = head // (AHEADS // KVHEADS)
            mine = narrow if head % 2 == 0 else ~narrow
            lanes = slice(head // 2 * 128, (head // 2 + 1) * 128)
            keys = k_ref[kv_head, pl.ds(start, length), :]
            values = v_ref[kv_head, pl.ds(start, length), :]
            for strip in range(length // STRIP):
                rows = slice(strip * STRIP, (strip + 1) * STRIP)
                width = (strip + 1) * STRIP if diagonal else length
                q = q_ref[rows, lanes]
                scores = dot_nt(jnp.where(mine, q, jnp.zeros_like(q)), keys[:width]) + mask_ref[rows, :width]
                old = top_ref[head, rows, :]
                new = jnp.maximum(old, jnp.max(scores, axis=1, keepdims=True))
                fade = jnp.exp(old - new)
                probs = jnp.exp(scores - new[:, :1])
                sum_ref[head, rows, :] = sum_ref[head, rows, :] * fade + jnp.sum(probs, axis=1, keepdims=True)
                top_ref[head, rows, :] = new
                acc = acc_ref[rows, lanes]
                acc_ref[rows, lanes] = jnp.where(mine, acc * fade + dot_nn(probs.astype(BF16), values[:width]), acc)
        return carry

    block(0, 0, diagonal=True)
    lax.fori_loop(1, rank + 1, block, 0)
    lane = lax.broadcasted_iota(jnp.int32, (length, 128), 1)
    stats = jnp.zeros((length, 128), F32)
    low = lane_is_low(length)
    for pair in range(AHEADS // 2):
        lanes = slice(pair * 128, (pair + 1) * 128)
        o_ref[:, lanes] = acc_ref[:, lanes] / jnp.where(low, sum_ref[2 * pair], sum_ref[2 * pair + 1])
    for head in range(AHEADS):
        stats = jnp.where(lane == head, top_ref[head] + jnp.log(sum_ref[head]), stats)
    lse_ref[...] = stats.T


def attend(rank, q, keyvals, seg_col, seg_blocks):
    length, total = q.shape[0], keyvals.shape[0]
    vmem = pl.BlockSpec(memory_space=pltpu.VMEM)
    return pl.pallas_call(
        attend_kernel,
        in_specs=[pl.BlockSpec(memory_space=pltpu.SMEM)] + [vmem] * 4,
        out_specs=[vmem, vmem],
        out_shape=[
            jax.ShapeDtypeStruct((length, QWIDTH), F32),
            jax.ShapeDtypeStruct((128, length), F32),
        ],
        scratch_shapes=[
            pltpu.VMEM((AHEADS, length, 128), F32),
            pltpu.VMEM((AHEADS, length, 128), F32),
            pltpu.VMEM((length, QWIDTH), F32),
            pltpu.VMEM((length, length), F32),
            pltpu.VMEM((KVHEADS, total, 128), BF16),
            pltpu.VMEM((KVHEADS, total, 128), BF16),
        ],
        compiler_params=PARAMS,
        cost_estimate=SHORT,
        name="attend",
    )(rank, q, keyvals, seg_col, seg_blocks)


def attend_backward_kernel(
    rank_ref, q_ref, kv_ref, do_ref, lse_ref, delta_ref, segq_ref, segk_ref, dq_ref, dkv_ref, k_ref, v_ref
):
    length = q_ref.shape[0]
    repeat_heads(kv_ref, k_ref, v_ref)
    rank = rank_ref[0]
    dq_ref[...] = jnp.zeros_like(dq_ref)
    dkv_ref[...] = jnp.zeros_like(dkv_ref)
    narrow = lane_is_low(STRIP)
    per = AHEADS // KVHEADS

    def strip_of(step, carry):
        start = pl.multiple_of(step * STRIP, STRIP)
        s = lax.broadcasted_iota(jnp.int32, (STRIP, length), 0) + start
        t = lax.broadcasted_iota(jnp.int32, (STRIP, length), 1) + rank * length
        seen = (s <= t) & (segk_ref[pl.ds(start, STRIP), :] == segq_ref[...])
        mask = jnp.where(seen, 0.0, NEGATIVE)
        sums = []
        for kv_head in range(KVHEADS):
            keys = k_ref[kv_head, pl.ds(start, STRIP), :]
            values = v_ref[kv_head, pl.ds(start, STRIP), :]
            dk = jnp.zeros((STRIP, 128), F32)
            dv = jnp.zeros((STRIP, 128), F32)
            for head in range(kv_head * per, (kv_head + 1) * per):
                mine = narrow if head % 2 == 0 else ~narrow
                lanes = slice(head // 2 * 128, (head // 2 + 1) * 128)
                q = q_ref[:, lanes]
                do = do_ref[:, lanes]
                own_keys = jnp.where(mine, keys, jnp.zeros_like(keys))
                own_values = jnp.where(mine, values, jnp.zeros_like(values))
                probs = jnp.exp(dot_nt(own_keys, q) + mask - lse_ref[head : head + 1, :])
                dp = dot_nt(own_values, do)
                ds = (probs * (dp - delta_ref[head : head + 1, :])).astype(BF16)
                dv += jnp.where(mine, dot_nn(probs.astype(BF16), do), 0.0)
                dk += jnp.where(mine, dot_nn(ds, q), 0.0)
                dq_ref[:, lanes] += dot_tn(ds, own_keys)
            sums.append((dk + pltpu.roll(dk, AHDIM, 1), dv + pltpu.roll(dv, AHDIM, 1)))
        dkv_ref[pl.ds(start, STRIP), :KWIDTH] = jnp.where(narrow, sums[0][0], sums[1][0])
        dkv_ref[pl.ds(start, STRIP), KWIDTH:] = jnp.where(narrow, sums[0][1], sums[1][1])
        return carry

    lax.fori_loop(0, (rank + 1) * (length // STRIP), strip_of, 0)


def attend_backward(rank, q, keyvals, do, lse, delta, seg_row, seg_keys):
    length, total = q.shape[0], keyvals.shape[0]
    vmem = pl.BlockSpec(memory_space=pltpu.VMEM)
    return pl.pallas_call(
        attend_backward_kernel,
        in_specs=[pl.BlockSpec(memory_space=pltpu.SMEM)] + [vmem] * 7,
        out_specs=[vmem, vmem],
        out_shape=[
            jax.ShapeDtypeStruct((length, QWIDTH), F32),
            jax.ShapeDtypeStruct((total, 2 * KWIDTH), F32),
        ],
        scratch_shapes=[
            pltpu.VMEM((KVHEADS, total, 128), BF16),
            pltpu.VMEM((KVHEADS, total, 128), BF16),
        ],
        compiler_params=PARAMS,
        cost_estimate=SHORT,
        name="attend_backward",
    )(rank, q, keyvals, do, lse, delta, seg_row, seg_keys)


def gather_keyvals(own):
    count = lax.axis_size("seq")
    if count == 2:
        got = lax.ppermute(own, "seq", [(0, 1)])
        first = lax.axis_index("seq") == 0
        return jnp.concatenate([jnp.where(first, own, got), own])
    return lax.all_gather(own, "seq", axis=0, tiled=True)


def scatter_keyval_grads(grads, length):
    count = lax.axis_size("seq")
    place = lax.axis_index("seq")
    if count == 2:
        own = lax.dynamic_slice_in_dim(grads, place * length, length)
        return own, lax.ppermute(grads[:length].astype(BF16), "seq", [(1, 0)])
    total = lax.psum_scatter(grads.astype(BF16), "seq", scatter_dimension=0, tiled=True)
    return jnp.zeros((length, grads.shape[1]), F32), total


def fit(value, rows):
    flat = value.reshape(-1)
    columns = -(-flat.shape[0] // rows)
    return jnp.pad(flat, (0, rows * columns - flat.shape[0])).reshape(rows, columns)


def on_device(
    tokens,
    segment_ids,
    norm1_gain,
    w_mamba_in,
    w_delta,
    conv_weight,
    conv_bias,
    delta_bias,
    decay_log,
    skip_gain,
    w_mamba_out,
    w_qkv,
    w_attn_out,
    norm2_gain,
    w_gate_up,
    w_down,
    cotangent,
):
    order_x, order_y = bit_orders()
    count = lax.axis_size("dp") * lax.axis_size("seq")
    rows = w_qkv.shape[0]
    width = rows * count
    taps_count, channels = conv_weight.shape
    conv_cols = -(-taps_count * channels // rows)
    bias_cols = -(-channels // rows)
    small = jnp.concatenate(
        [w_delta, norm1_gain[:, None], norm2_gain[:, None], fit(conv_weight, rows), fit(conv_bias, rows)], axis=1
    )
    small_width = 128 * (-(-small.shape[1] // 128))
    small = jnp.pad(small, ((0, 0), (0, small_width - small.shape[1])))

    packed = jnp.concatenate([w_mamba_in, w_qkv, small], axis=1)
    w_in = lax.all_gather(packed, ("dp", "seq"), axis=0, tiled=True)
    second = [Doubling(w_mamba_out, order_x), Doubling(w_attn_out, order_y)]
    third = Doubling(w_down, order_y)
    while len(third.todo) > 2:
        step((), *second, third)
    finish(*second)
    w_mo, w_ao = (chain.whole() for chain in second)
    gate_up = lax.all_gather(w_gate_up, ("dp", "seq"), axis=0, tiled=True)
    mamba_width = w_mamba_in.shape[1]
    w_z, w_x, w_q = w_in[:, :INNER], w_in[:, INNER:mamba_width], w_in[:, mamba_width:]

    smalls = w_q[:, QWIDTH + 2 * KWIDTH :]
    gain_one = smalls[:, MHEADS].astype(F32)
    gain_two = smalls[:, MHEADS + 1].astype(F32)
    at = MHEADS + 2
    conv_kernel = smalls[:, at : at + conv_cols].reshape(count, rows * conv_cols)[:, : taps_count * channels]
    conv_kernel = conv_kernel.reshape(count, taps_count, channels).transpose(1, 0, 2)
    conv_kernel = conv_kernel.reshape(taps_count, count * channels).astype(F32)
    at += conv_cols
    conv_shift = smalls[:, at : at + bias_cols].reshape(count, rows * bias_cols)[:, :channels]
    conv_shift = conv_shift.reshape(count * channels).astype(F32)

    length = tokens.shape[1]
    seg_full = segment_ids[0]
    total = seg_full.shape[0]
    rank = lax.axis_index("seq")
    first_row = rank * length
    back = taps_count - 1
    seg_padded = jnp.concatenate([jnp.full((back,), -1, jnp.int32), seg_full])
    seg_own = lax.dynamic_slice_in_dim(seg_full, first_row, length)
    seg_before = lax.dynamic_slice_in_dim(seg_padded, first_row + back - 1, 1)[0]
    taps = [
        (lax.dynamic_slice_in_dim(seg_padded, first_row + back - j, length) == seg_own).astype(F32)[:, None]
        for j in range(taps_count)
    ]
    seg_col = seg_own[:, None]
    seg_row = seg_own[None, :]
    rank_arg = rank.astype(jnp.int32).reshape(1)

    inputs = tokens[0].astype(F32)
    r1 = lax.rsqrt(jnp.mean(inputs * inputs, axis=-1, keepdims=True) + EPSILON)
    n1 = (inputs * r1 * gain_one[None, :]).astype(BF16)
    n1, w_mo, w_ao = step((n1, w_mo, w_ao), third)
    qkv_small = dot_nn(n1, w_q)
    qkv = qkv_small[:, : QWIDTH + 2 * KWIDTH]
    delta_raw = qkv_small[:, QWIDTH + 2 * KWIDTH : QWIDTH + 2 * KWIDTH + 128]
    xbc = dot_nn(n1, w_x).astype(BF16)
    z = dot_nn(n1, w_z).astype(BF16)


    freqs = ROPE_BASE ** (-(jnp.arange(AHDIM // 2).astype(F32) * 2.0 / AHDIM))
    angles = (first_row + jnp.arange(length, dtype=jnp.int32)).astype(F32)[:, None] * freqs[None, :]
    cosine = jnp.tile(jnp.cos(angles), (1, 4))
    sine_half = jnp.sin(angles)
    sine = jnp.tile(jnp.concatenate([-sine_half, sine_half], axis=1), (1, 2))
    q, keyvals = rope(qkv, cosine, sine)
    all_keyvals = gather_keyvals(keyvals)

    halo = jnp.pad(neighbour(xbc[length - back :], 1).astype(F32), ((8 - back, 0), (0, 0)))
    kernel_wide = jnp.concatenate([conv_kernel, conv_shift[None, :]])
    kernel_wide = jnp.pad(kernel_wide, ((0, 7 - taps_count), (0, 0)))
    taps_wide = jnp.pad(jnp.concatenate(taps, axis=1), ((0, 0), (0, 8 - taps_count)))
    u = conv_forward(xbc, halo, kernel_wide, taps_wide, taps_count)

    heads = jnp.stack([delta_bias, decay_log]).astype(F32)
    heads = jnp.pad(heads, ((0, 6), (0, 128 - MHEADS)))
    vec, row = heads_forward(seg_before.reshape(1), delta_raw, heads, seg_col)
    gate_lanes = jnp.repeat(vec[3, -1, :MHEADS], MHDIM)
    skip_lanes = jnp.repeat(skip_gain.astype(F32), MHDIM)[None, :]

    y_local, state_part = ssd_forward(u, u, u, vec, row, seg_col, seg_row)
    state_in = state_from_behind(gate_lanes, state_part)

    q, _ = tie(q, state_part)
    attended, lse = attend(rank_arg, q, all_keyvals, seg_col, seg_full.reshape(total // length, length))
    attended_low = attended.astype(BF16)

    y, mixed_low = ssd_finish(y_local, u, z, u, state_in, vec, skip_lanes)
    mixed_low = step(mixed_low, third)
    residual = inputs + dot_nn(mixed_low, w_mo) + dot_nn(attended_low, w_ao)

    r2 = lax.rsqrt(jnp.mean(residual * residual, axis=-1, keepdims=True) + EPSILON)
    n2 = (residual * r2 * gain_two[None, :]).astype(BF16)
    gu = dot_nn(n2, gate_up)
    gu = step(gu, third)
    down = third.whole()
    half = gu.shape[1] // 2
    gate, up = gu[:, :half], gu[:, half:]
    gate_act, gate_slope = silu_parts(gate)
    hidden = (gate_act * up).astype(BF16)
    upstream_low = cotangent[0]
    upstream = upstream_low.astype(F32)
    sum_down = Halving(dot_tn(hidden, upstream_low).astype(BF16), order_x)
    hidden = step(hidden, sum_down)
    block_out = (residual + dot_nn(hidden, down)).astype(BF16)
    upstream_low, block_out = step((upstream_low, block_out), sum_down)
    dhidden = dot_nt(upstream_low, down)
    dgate = (dhidden * up * gate_slope).astype(BF16)
    dup = (dhidden * gate_act).astype(BF16)
    dgu = jnp.concatenate([dgate, dup], axis=1)
    grad_gate_up = dot_tn(n2, dgu).astype(BF16)
    dgu, grad_gate_up = tie(dgu, grad_gate_up)
    grad_gate_up = lax.psum_scatter(grad_gate_up, ("dp", "seq"), scatter_dimension=0, tiled=True).astype(F32)
    dn2 = dot_nt(dgu, gate_up)
    scaled = gain_two[None, :] * dn2
    grad_gain_two = jnp.sum(dn2 * residual * r2, axis=0)
    dhs = upstream + r2 * scaled - residual * (r2 * r2 * r2) * jnp.mean(scaled * residual, axis=-1, keepdims=True)
    dhs_low = dhs.astype(BF16)
    dym = dot_nt(dhs_low, w_mo)
    do = dot_nt(dhs_low, w_ao).astype(BF16)
    sum_mo = Halving(dot_tn(mixed_low, dhs_low).astype(BF16), order_y)
    sum_ao = Halving(dot_tn(attended_low, dhs_low).astype(BF16), order_x)
    dym, do = step((dym, do), sum_mo, sum_ao)

    dy, dz, dstate_part, skip_cols = ssd_gate(dym, y, u, z, u, vec)
    dstate = state_from_ahead(gate_lanes, dstate_part)
    dz, dy = step((dz, dy), sum_down, sum_mo, sum_ao)
    sum_z = Halving(dot_tn(n1, dz).astype(BF16), order_y)
    dy = step(dy, sum_z)

    dx, db, dc, cols, rows_sum = ssd_backward(
        u, dy, u, u, state_in, dstate, vec, row, seg_row.T, seg_row, skip_lanes
    )
    cols, rows_sum, dx = step((cols, rows_sum, dx), sum_down, sum_ao, sum_mo, sum_z)
    ddelta_low, head_sums = heads_backward(delta_raw, heads, cols, rows_sum, skip_cols)
    sum_heads = Summing(head_sums)

    dxbc, last_rows, spilled, conv_grads = conv_backward(dx, db, dc, xbc, halo, kernel_wide, taps_wide, taps_count)
    incoming = jnp.pad(neighbour(spilled[8 - back :], -1), ((8 - back, 0), (0, 0)))
    dxbc, last_rows = step((dxbc, last_rows), sum_down, sum_ao)
    dxbc = lax.dynamic_update_slice_in_dim(dxbc, (last_rows + incoming).astype(BF16), length - 8, 0)
    cut = 640
    sum_x = [
        Halving(dot_tn(n1, dxbc[:, :cut]).astype(BF16), order_y),
        Halving(dot_tn(n1, dxbc[:, cut : 2 * cut]).astype(BF16), order_x),
        Halving(dot_tn(n1, dxbc[:, 2 * cut :]).astype(BF16), order_x),
    ]
    do = step(do, *sum_x, sum_heads)

    owner = (jnp.arange(QWIDTH)[None, :] // AHDIM == jnp.arange(AHEADS)[:, None]).astype(F32)
    delta = lax.dot_general(
        owner, do.astype(F32) * attended, (((1,), (1,)), ((), ())), precision=lax.Precision.HIGHEST
    )
    do, delta = step((do, delta), *sum_x, sum_mo, sum_z)
    dq, dkv = attend_backward(
        rank_arg, q, all_keyvals, do, lse, delta, seg_row, seg_full[:, None]
    )
    dq, dkv = step((dq, dkv), *sum_x, sum_heads, sum_z, sum_mo, sum_ao, sum_down)
    own_dkv, more_dkv = scatter_keyval_grads(dkv, length)
    dqkv = unrope(dq, own_dkv, more_dkv, cosine, sine)
    sum_qkv = Halving(dot_tn(n1, dqkv).astype(BF16), order_y)
    dqkv = step(dqkv, *sum_x, sum_heads, sum_z, sum_mo, sum_ao, sum_qkv)

    kernel_grad = conv_grads[:taps_count].reshape(taps_count, count, channels).transpose(1, 0, 2)
    kernel_grad = kernel_grad.reshape(count, taps_count * channels)
    shift_grad = conv_grads[taps_count].reshape(count, channels)
    def fit_all(value, columns):
        spare = rows * columns - value.shape[1]
        return jnp.pad(value, ((0, 0), (0, spare))).reshape(width, columns)

    ddelta_wide = jnp.pad(ddelta_low, ((0, 0), (0, small_width - 128)))
    dq_small = jnp.concatenate([dqkv, ddelta_wide], axis=1)
    dn1 = dot_nt(dq_small, w_q) + dot_nt(dz, w_z) + dot_nt(dxbc, w_x)
    scaled = gain_one[None, :] * dn1
    grad_gain_one = jnp.sum(dn1 * inputs * r1, axis=0)
    grad_tokens = dhs + r1 * scaled - inputs * (r1 * r1 * r1) * jnp.mean(scaled * inputs, axis=-1, keepdims=True)

    parts = [
        dot_tn(n1, ddelta_low)[:, :MHEADS],
        grad_gain_one[:, None],
        grad_gain_two[:, None],
        fit_all(kernel_grad, conv_cols),
        fit_all(shift_grad, bias_cols),
    ]
    used = sum(p.shape[1] for p in parts)
    parts.append(jnp.zeros((width, small_width - used), F32))
    small_sum = jnp.concatenate(parts, axis=1).astype(BF16).reshape(count, rows, small_width)
    small_sum = lax.all_to_all(small_sum, ("dp", "seq"), 0, 0, tiled=True)
    grad_small = jnp.sum(small_sum.astype(F32), axis=0)
    finish(sum_z, sum_qkv, sum_mo, sum_ao, sum_down, sum_heads, *sum_x)
    grad_x = jnp.concatenate([chain.value for chain in sum_x], axis=1)
    head_grads = sum_heads.value

    at = MHEADS + 2
    kernel_own = grad_small[:, at : at + conv_cols].reshape(-1)[: taps_count * channels].reshape(taps_count, channels)
    at += conv_cols
    shift_own = grad_small[:, at : at + bias_cols].reshape(-1)[:channels]
    return (
        block_out[None],
        grad_tokens[None],
        grad_small[:, MHEADS],
        jnp.concatenate([sum_z.value, grad_x], axis=1),
        grad_small[:, :MHEADS],
        kernel_own,
        shift_own,
        head_grads[0, :MHEADS],
        head_grads[1, :MHEADS],
        head_grads[2, :MHEADS],
        sum_mo.value,
        sum_qkv.value,
        sum_ao.value,
        grad_small[:, MHEADS + 1],
        grad_gate_up,
        sum_down.value,
    )


def solution(mesh):
    both = ("dp", "seq")
    in_specs = (
        P("dp", "seq", None),
        P("dp", None),
        P(both),
        P(both, None),
        P(both, None),
        P(None, both),
        P(both),
        P(),
        P(),
        P(),
        P(both, None),
        P(both, None),
        P(both, None),
        P(both),
        P(both, None),
        P(both, None),
        P("dp", "seq", None),
    )
    out_specs = (
        P("dp", "seq", None),
        P("dp", "seq", None),
        P(both),
        P(both, None),
        P(both, None),
        P(None, both),
        P(both),
        P(),
        P(),
        P(),
        P(both, None),
        P(both, None),
        P(both, None),
        P(both),
        P(both, None),
        P(both, None),
    )
    return jax.shard_map(
        on_device, mesh=mesh, in_specs=in_specs, out_specs=out_specs, check_vma=False
    )
```
